512 devices in a mesh: section: 8 (over x, z_hi), seq: 64 (over y, z_lo, core).
Axes of the slice: x: 4, y: 4, z: 16 (z_hi: 2, z_lo: 8; z = z_hi * 8 + z_lo), core: 2. Of those that a mesh axis runs over, the one named last changes fastest.
Arguments:
- queries: bfloat16 [8, 256, 2048], P('section', 'seq'), may hold values from -120 to 120
- keys_values: bfloat16 [8, 16384, 4096], P('section', 'seq'), may hold values from -41 to 41
- enc_len: int32 [8], P('section'), may hold values from 4096 to 16384, as said below
- order: int32 [8], replicated, may hold values from 0 to 7, each once
- d_out: bfloat16 [8, 256, 2048], P('section', 'seq'), may hold values from -6 to 6
Outputs:
- attended: bfloat16 [8, 256, 2048], P('section', 'seq')
- d_queries: bfloat16 [8, 256, 2048], P('section', 'seq')
- d_keys_values: bfloat16 [8, 16384, 4096], P('section', 'seq')
The draws below stay inside these ranges and needn't reach their ends.
Inputs may be any that keep to these rules, and one draw needn't show every extreme that they name: Positions from enc_len on are padding; some micro-batch has exactly 16384 valid positions. `order`: every micro-batch is run by exactly one group.
All inputs are finite; a program needn't handle non-finite values.
Results may differ from the reference program's by a relative error of at most 0.0049.
Values may be sent and summed in bfloat16 or wider, within the bound.
A program may use at most 64 MiB of HBM per device.

```python
import math
import jax
import jax.numpy as jnp
from jax import lax

H = 8
HD = 256
SD = 256
SE = 16384
DA = 2048
N_SECTION = 8


def draw_queries(key, part):
    shape = (N_SECTION, SD, H * HD)
    first_key = jax.random.fold_in(jax.random.fold_in(key, 11), 0)
    values = jax.random.truncated_normal(first_key, -6.0, 6.0, shape, jnp.float32)
    return values.astype(jnp.bfloat16)


def draw_keys_values(key, part):
    shape = (N_SECTION, SE, 2 * H * HD)
    first_key = jax.random.fold_in(jax.random.fold_in(key, 23), 0)
    values = jax.random.truncated_normal(first_key, -6.0, 6.0, shape, jnp.float32)
    return values.astype(jnp.bfloat16)


def draw_enc_len(key, part):
    first_key, second_key = jax.random.split(jax.random.fold_in(key, 37))
    drawn = jax.random.randint(first_key, (N_SECTION,), SE // 4, SE + 1, jnp.int32)
    full_spot = jax.random.randint(second_key, (), 0, N_SECTION, jnp.int32)
    return jnp.where(jnp.arange(N_SECTION, dtype=jnp.int32) == full_spot, SE, drawn).astype(jnp.int32)


def levels(key, dims, cuts, smallest, top_value):
    factor_of, own = 1.0, jax.random.fold_in(key, 6)
    for dim, shards_of in cuts:
        heights = jnp.exp(jax.random.uniform(jax.random.fold_in(own, dim), (shards_of,), jnp.float32, smallest / len(cuts), top_value / len(cuts)))
        factor_of = factor_of * jnp.repeat(heights, dims[dim] // shards_of).reshape([-1 if axis == dim else 1 for axis in range(len(dims))])
    return factor_of


def normal_values(rng, dims, scale, reach, pieces=(), held_as=jnp.bfloat16):
    entries = jax.random.normal(rng, dims, jnp.float32) * scale
    if len(pieces) > 0:
        entries = levels(rng, dims, pieces, -0.22, 0.18) * entries
    return jnp.clip(entries, min=-reach, max=reach).astype(held_as)


def setup_inputs(seed: int = 0) -> dict:
    seeds = jax.random.split(jax.random.key(seed), 6)
    queries = draw_queries(jax.random.fold_in(seeds[5], 71), 0)
    keys_values = draw_keys_values(jax.random.fold_in(seeds[5], 71), 0)
    enc_len = draw_enc_len(jax.random.fold_in(seeds[5], 71), 0)
    order = jax.random.permutation(seeds[3], N_SECTION).astype(jnp.int32)
    d_out = normal_values(seeds[4], (N_SECTION, SD, DA), 1.0, 6.0, ((0, 8), (1, 64)))
    return {"queries": queries, "keys_values": keys_values, "enc_len": enc_len, "order": order, "d_out": d_out}


def group_pass(query_rows, grad_rows, memory, length):
    score_scale = 1.0 / math.sqrt(HD)
    key_count = memory.shape[0]
    attn_width = H * HD
    key_heads = memory[:, :attn_width].reshape(key_count, H, HD).astype(jnp.float32)
    value_heads = memory[:, attn_width:].reshape(key_count, H, HD).astype(jnp.float32)
    key_valid = jnp.arange(key_count, dtype=jnp.int32) < length
    block_rows = math.gcd(SD, 256)

    def step(totals, inputs):
        query_block, grad_block = inputs
        query_heads = query_block.reshape(block_rows, H, HD).astype(jnp.float32)
        grad_heads = grad_block.reshape(block_rows, H, HD).astype(jnp.float32)
        scores = jnp.einsum('ihd,jhd->hij', query_heads, key_heads) * score_scale
        scores = jnp.where(key_valid[None, None, :], scores, -jnp.inf)
        row_max = lax.optimization_barrier(jnp.max(scores, axis=-1, keepdims=True))
        shifted = jnp.exp(scores - row_max)
        probabilities = shifted / lax.optimization_barrier(jnp.sum(shifted, axis=-1, keepdims=True))
        weights = probabilities.astype(jnp.bfloat16)
        attended = jnp.einsum('hij,jhd->ihd', weights.astype(jnp.float32), value_heads)
        attended = attended.reshape(block_rows, attn_width).astype(jnp.bfloat16)
        dprobs = jnp.einsum('ihd,jhd->hij', grad_heads, value_heads)
        row_delta = lax.optimization_barrier(jnp.sum(probabilities * dprobs, axis=-1, keepdims=True))
        dscores = (probabilities * (dprobs - row_delta) * score_scale).astype(jnp.bfloat16)
        query_grad = jnp.einsum('hij,jhd->ihd', dscores.astype(jnp.float32), key_heads)
        query_grad = query_grad.reshape(block_rows, attn_width).astype(jnp.bfloat16)
        key_grad = jnp.einsum('hij,ihd->jhd', dscores.astype(jnp.float32), query_heads)
        value_grad = jnp.einsum('hij,ihd->jhd', weights.astype(jnp.float32), grad_heads)
        return ((totals[0] + key_grad, totals[1] + value_grad), (attended, query_grad))
    query_blocks = query_rows.reshape(SD // block_rows, block_rows, attn_width)
    grad_blocks = grad_rows.reshape(SD // block_rows, block_rows, attn_width)
    zero_grads = jnp.zeros((key_count, H, HD), jnp.float32)
    totals, outputs = lax.scan(step, (zero_grads, zero_grads), (query_blocks, grad_blocks))
    joined = jnp.concatenate([totals[0].reshape(key_count, attn_width), totals[1].reshape(key_count, attn_width)], axis=1)
    return (outputs[0].reshape(SD, attn_width), outputs[1].reshape(SD, attn_width), joined.astype(jnp.bfloat16))

def reference(queries, keys_values, enc_len, order, d_out):
    attended_list = []
    query_list = []
    grads_all = jnp.zeros((N_SECTION, SE, 2 * H * HD), jnp.bfloat16)
    for group_index in range(N_SECTION):
        planned = order[group_index].astype(jnp.int32)
        memory = lax.dynamic_index_in_dim(keys_values, planned, 0, keepdims=False)
        length = lax.dynamic_index_in_dim(enc_len, planned, 0, keepdims=False)
        attended_g, query_grad_g, joined_g = group_pass(queries[group_index], d_out[group_index], memory, length)
        attended_list.append(attended_g)
        query_list.append(query_grad_g)
        grads_all = grads_all.at[planned].set(joined_g)
    return (jnp.stack(attended_list), jnp.stack(query_list), grads_all)
```

```python
import functools
import math

import jax
import jax.numpy as jnp
from jax import lax
from jax.experimental import pallas as pl
from jax.experimental.pallas import tpu as pltpu
from jax.sharding import PartitionSpec as P

MESH = pl.DeviceIdType.MESH
HD = 256
NX, NY, NZ = 4, 4, 8
BF = jnp.bfloat16
F32 = jnp.float32


def mod(a, n):
    return lax.rem(a, jnp.int32(n))


def merge(parts):
    top = functools.reduce(jnp.maximum, [p[0] for p in parts])
    scale = [jnp.exp(p[0] - top) for p in parts]
    total = sum(p[1] * s for p, s in zip(parts, scale))
    dots = sum(p[2] * s for p, s in zip(parts, scale))
    return top, total, dots


def kernel(
    q_ref, kv_ref, len_ref, ord_ref, g_ref,
    att_ref, dq_ref, dkv_ref,
    qv, xb0, xb1, rows8, sb, own, pb, gb, dense, kvv, ev, dv,
    st, sy, szc, szq, st2, st3,
    wv, dsv, of, sd, sd2, rr, ry, ys, zs, zq, zt, zc, rt, rb0, rb1, psd, prb, dkvs,
    load_sem, xs_sem, xr_sem, kvs_sem, kvr_sem, ps_sem, pr_sem, zs_sem, zr_sem,
    ys_sem, yr_sem, ss_sem, sr_sem, as_sem, ar_sem, bs_sem, br_sem, ts_sem, tr_sem, ds_sem, dr_sem,
):
    sec = lax.axis_index("section")
    seq = lax.axis_index("seq")
    x, h = lax.div(sec, jnp.int32(2)), mod(sec, 2)
    y, zl, c = lax.div(seq, jnp.int32(16)), mod(lax.div(seq, jnp.int32(2)), NZ), mod(seq, 2)
    xb, rb = (xb0, xb1), (rb0, rb1)
    half = att_ref.shape[2] // 2
    heads = half // HD
    keys = kv_ref.shape[1]
    width = half * 2
    score_scale = 1.0 / math.sqrt(HD)
    quad, zin = lax.div(zl, jnp.int32(4)) * 4, mod(zl, 4)
    zx = mod(zl + 4, NZ)

    def dev(xx, hh, yy, zz, cc):
        return (xx * 2 + hh, (yy * NZ + zz) * 2 + cc)

    def zto(d):
        return quad + mod(zin + d, 4)

    def zfrom(d):
        return quad + mod(zin + 4 - d, 4)

    def slot(r):
        base = zfrom(r % 4)
        return base if r < 4 else mod(base + 4, NZ)

    def ynb(d):
        return mod(y + d + NY, NY)

    other = 1 - c
    core_of = lambda dc: c if dc == 0 else other
    x_peers = [(dx, dc) for dx in range(NX) for dc in range(2) if dx or dc]
    partner = dev(x, 1 - h, y, zx, c)
    pending = []

    def send(src, dst, ssem, rsem, target):
        copy = pltpu.make_async_remote_copy(
            src_ref=src, dst_ref=dst, send_sem=ssem, recv_sem=rsem, device_id=target, device_id_type=MESH
        )
        copy.start()
        pending.append(copy)

    def arrive(dst, ssem, rsem):
        pltpu.make_async_remote_copy(
            src_ref=dst, dst_ref=dst, send_sem=ssem, recv_sem=rsem, device_id=partner, device_id_type=MESH
        ).wait_recv()

    barrier = pltpu.get_barrier_semaphore()
    peers = [dev(mod(x + dx, NX), h, y, zl, core_of(dc)) for dx, dc in x_peers]
    peers += [dev(x, h, ynb(d), zl, c) for d in (1, 2, -1)]
    peers += [dev(x, h, y, zto(d), c) for d in (1, 2, 3)]
    peers += [dev(x, h, y, zx, c), partner]
    for peer in peers:
        pl.semaphore_signal(barrier, inc=1, device_id=peer, device_id_type=MESH)
    load_q = [
        pltpu.make_async_copy(ref.at[0], qv.at[a], load_sem.at[a]) for a, ref in enumerate((q_ref, g_ref))
    ]
    for copy in load_q:
        copy.start()
    my_cols = [pl.multiple_of(b * width + c * half, HD) for b in range(2)]
    their_cols = [pl.multiple_of(b * width + other * half, HD) for b in range(2)]
    my_keys = pl.ds(pl.multiple_of(c * keys, keys), keys)
    load_kv = []
    for b in range(2):
        for n in range(heads):
            copy = pltpu.make_async_copy(
                kv_ref.at[0, :, pl.ds(my_cols[b] + n * HD, HD)], kvv.at[b, n, my_keys], load_sem.at[2 + b * heads + n]
            )
            copy.start()
            load_kv.append(copy)
    for copy in load_q:
        copy.wait()
    pl.semaphore_wait(barrier, len(peers))

    for a in range(2):
        for dx, dc in x_peers:
            k = dx * 2 + dc
            cc = core_of(dc)
            send(
                qv.at[a, :, pl.ds(pl.multiple_of(cc * half, half), half)],
                xb[a].at[k], xs_sem.at[k, a], xr_sem.at[k, a],
                dev(mod(x + dx, NX), h, y, zl, cc),
            )
    own_copy = [
        pltpu.make_async_copy(
            qv.at[a, :, pl.ds(pl.multiple_of(c * half, half), half)], xb[a].at[0], load_sem.at[2 + 4 * heads + a]
        )
        for a in range(2)
    ]
    for copy in own_copy:
        copy.start()
    for b in range(2):
        for n in range(heads):
            send(
                kv_ref.at[0, :, pl.ds(their_cols[b] + n * HD, HD)], kvv.at[b, n, my_keys],
                kvs_sem.at[b, n], kvr_sem.at[b, n], dev(x, h, y, zl, other),
            )

    def inverse(section):
        found = jnp.int32(0)
        for k in range(2 * NX):
            found = jnp.where(ord_ref[k] == section, jnp.int32(k), found)
        return found

    twin = x * 2 + (1 - h)
    src_mine, src_twin = inverse(sec), inverse(twin)

    def pick(section, a):
        k = mod(x - lax.div(section, jnp.int32(2)) + NX, NX) * 2
        rows8[0:4, :] = xb[a][k + c].astype(F32)
        rows8[4:8, :] = xb[a][k + other].astype(F32)
        return rows8[...].astype(BF)

    for a in range(2):
        own_copy[a].wait()
        for dx, dc in x_peers:
            k = dx * 2 + dc
            arrive(xb[a].at[k], xs_sem.at[k, a], xr_sem.at[k, a])
        sb[a] = pick(src_twin, a)
        send(sb.at[a], pb.at[a], ps_sem.at[a], pr_sem.at[a], partner)
    for a in range(2):
        own[a] = pick(src_mine, a)
    mine_here = mod(src_mine, 2) == h

    def to_quad(r, a):
        b = r // 4
        for d in (1, 2, 3):
            send(
                gb.at[y, slot(r), a], gb.at[y, slot(r), a], zs_sem.at[d + 4 * b, a], zr_sem.at[d + 4 * b, a],
                dev(x, h, y, zto(d), c),
            )

    def to_y(r, a):
        for i, d in enumerate((1, -1)):
            send(
                gb.at[y, slot(r), a], gb.at[y, slot(r), a], ys_sem.at[i, r, a], yr_sem.at[i, r, a],
                dev(x, h, ynb(d), zl, c),
            )

    def relay_y(r, a):
        d = 1 if a == 0 else -1
        arrive(gb.at[ynb(-d), slot(r), a], ys_sem.at[a, r, a], yr_sem.at[a, r, a])
        send(
            gb.at[ynb(-d), slot(r), a], gb.at[ynb(-d), slot(r), a], ys_sem.at[2, r, a], yr_sem.at[2, r, a],
            dev(x, h, ynb(d), zl, c),
        )

    def z_arrive(r, a):
        arrive(gb.at[y, slot(r), a], zs_sem.at[r, a], zr_sem.at[r, a])

    for a in range(2):
        arrive(pb.at[a], ps_sem.at[a], pr_sem.at[a])
        gb[y, zl, a] = jnp.where(mine_here, own[a], pb[a])
        send(gb.at[y, zl, a], gb.at[y, zl, a], zs_sem.at[4, a], zr_sem.at[4, a], dev(x, h, y, zx, c))
        to_quad(0, a)
        to_y(0, a)
    for a in range(2):
        z_arrive(4, a)
        to_quad(4, a)
        to_y(4, a)
    for r in (1, 2, 3):
        for a in range(2):
            z_arrive(r, a)
            to_y(r, a)
    for r in (0, 4):
        for a in range(2):
            relay_y(r, a)
    for r in (5, 6, 7):
        for a in range(2):
            z_arrive(r, a)
            to_y(r, a)
    for r in (1, 2, 3, 5, 6, 7):
        for a in range(2):
            relay_y(r, a)
    for copy in load_kv:
        copy.wait()
    for b in range(2):
        for n in range(heads):
            arrive(kvv.at[b, n, pl.ds(pl.multiple_of(other * keys, keys), keys)], kvs_sem.at[b, n], kvr_sem.at[b, n])
    for r in range(NZ):
        for a in range(2):
            i = 1 - a
            arrive(gb.at[ynb(1 if i else -1), slot(r), a], ys_sem.at[i, r, a], yr_sem.at[i, r, a])
            arrive(gb.at[ynb(2), slot(r), a], ys_sem.at[2, r, a], yr_sem.at[2, r, a])

    first_key = (y * NZ + zl) * (2 * keys)
    key_at = lax.broadcasted_iota(jnp.int32, (2 * keys, HD), 0) + first_key
    valid = key_at < len_ref[0]
    nt = (((1,), (1,)), ((), ()))
    nn = (((1,), (0,)), ((), ()))
    tn = (((0,), (0,)), ((), ()))
    targets = NY * NZ * 8
    for n in range(heads):
        for a in range(2):
            block = gb[:, :, a, :, n * HD : (n + 1) * HD].astype(F32)
            dense[a, n] = block.reshape(targets, HD).astype(BF)
        scores = lax.dot_general(kvv[0, n], dense[0, n], nt, preferred_element_type=F32) * score_scale
        scores = jnp.where(valid, scores, -jnp.inf)
        top = jnp.maximum(jnp.max(scores, axis=0, keepdims=True), -1e30)
        e = jnp.exp(scores - top)
        dp = lax.dot_general(kvv[1, n], dense[1, n], nt, preferred_element_type=F32)
        ev[n] = e
        dv[n] = dp
        st[0, n : n + 1, :] = top
        st[1, n : n + 1, :] = jnp.sum(e, axis=0, keepdims=True)
        st[2, n : n + 1, :] = jnp.sum(e * dp, axis=0, keepdims=True)

    for i, d in enumerate((1, 2, -1)):
        send(st, sy.at[i], ss_sem.at[i], sr_sem.at[i], dev(x, h, ynb(d), zl, c))
    for i in range(3):
        arrive(sy.at[i], ss_sem.at[i], sr_sem.at[i])
    part = merge([(st[0], st[1], st[2])] + [(sy[i, 0], sy[i, 1], sy[i, 2]) for i in range(3)])
    for i in range(3):
        st2[i] = part[i]
    send(st2, szc, ss_sem.at[3], sr_sem.at[3], dev(x, h, y, zx, c))
    arrive(szc, ss_sem.at[3], sr_sem.at[3])
    part = merge([part, (szc[0], szc[1], szc[2])])
    for i in range(3):
        st3[i] = part[i]
    for d in (1, 2, 3):
        send(st3, szq.at[d - 1], ss_sem.at[3 + d], sr_sem.at[3 + d], dev(x, h, y, zto(d), c))
    for d in (1, 2, 3):
        arrive(szq.at[d - 1], ss_sem.at[3 + d], sr_sem.at[3 + d])
    whole_max, whole_sum, dots = merge([part] + [(szq[i, 0], szq[i, 1], szq[i, 2]) for i in range(3)])
    inv_sum = 1.0 / whole_sum
    delta = dots * inv_sum
    factor = jnp.exp(st[0] - whole_max) * inv_sum

    for n in range(heads):
        p = ev[n] * factor[n : n + 1, :]
        wv[n] = p.astype(BF)
        dsv[n] = (p * (dv[n] - delta[n : n + 1, :]) * score_scale).astype(BF)
        for a in range(2):
            d = 1 if a == 0 else -1
            out = lax.dot_general(
                (wv if a == 0 else dsv)[n], kvv[1 - a, n], tn, preferred_element_type=F32
            )
            of[a, n] = out.reshape(NY, NZ * 8, HD)
            sd[a, n, 0] = of[a, n, ynb(2)].astype(BF)
            send(sd.at[a, n, 0], rr.at[a, n], as_sem.at[a, n, 0], ar_sem.at[a, n, 0], dev(x, h, ynb(d), zl, c))
            sd[a, n, 1] = of[a, n, ynb(-d)].astype(BF)
            send(sd.at[a, n, 1], ry.at[a, n, 1], as_sem.at[a, n, 1], ar_sem.at[a, n, 1], dev(x, h, ynb(-d), zl, c))
    for n in range(heads):
        for a in range(2):
            d = 1 if a == 0 else -1
            arrive(rr.at[a, n], as_sem.at[a, n, 0], ar_sem.at[a, n, 0])
            sd2[a, n] = (rr[a, n].astype(F32) + of[a, n, ynb(d)]).astype(BF)
            send(sd2.at[a, n], ry.at[a, n, 0], as_sem.at[a, n, 2], ar_sem.at[a, n, 2], dev(x, h, ynb(d), zl, c))

    stores = []
    for n in range(heads):
        for b in range(2):
            grad = lax.dot_general((dsv, wv)[b][n], dense[b, n], nn, preferred_element_type=F32)
            dkvs[b, n] = grad.astype(BF)
            copy = pltpu.make_async_copy(
                dkvs.at[b, n, my_keys], dkv_ref.at[0, :, pl.ds(my_cols[b] + n * HD, HD)], load_sem.at[2 + 2 * heads + b * heads + n]
            )
            copy.start()
            stores.append(copy)
            send(
                dkvs.at[b, n, pl.ds(pl.multiple_of(other * keys, keys), keys)],
                dkv_ref.at[0, :, pl.ds(my_cols[b] + n * HD, HD)],
                ds_sem.at[b, n], dr_sem.at[b, n], dev(x, h, y, zl, other),
            )

    for a in range(2):
        for n in range(heads):
            arrive(ry.at[a, n, 0], as_sem.at[a, n, 2], ar_sem.at[a, n, 2])
            arrive(ry.at[a, n, 1], as_sem.at[a, n, 1], ar_sem.at[a, n, 1])
            total = of[a, n, y] + ry[a, n, 0].astype(F32) + ry[a, n, 1].astype(F32)
            ys[a, :, :, n * HD : (n + 1) * HD] = total.reshape(NZ, 8, HD)
        for d in (1, 2, 3):
            zs[a, d - 1, 0] = ys[a, zto(d)].astype(BF)
            zs[a, d - 1, 1] = ys[a, mod(zto(d) + 4, NZ)].astype(BF)
            send(zs.at[a, d - 1], zq.at[a, d - 1], bs_sem.at[a, d], br_sem.at[a, d], dev(x, h, y, zto(d), c))
    for a in range(2):
        for d in (1, 2, 3):
            arrive(zq.at[a, d - 1], bs_sem.at[a, d], br_sem.at[a, d])
        far = ys[a, zx] + sum(zq[a, i, 1].astype(F32) for i in range(3))
        zt[a] = far.astype(BF)
        send(zt.at[a], zc.at[a], bs_sem.at[a, 0], br_sem.at[a, 0], dev(x, h, y, zx, c))
    for a in range(2):
        near = ys[a, zl] + sum(zq[a, i, 0].astype(F32) for i in range(3))
        arrive(zc.at[a], bs_sem.at[a, 0], br_sem.at[a, 0])
        rows8[...] = near + zc[a].astype(F32)
        rt[0, a] = rows8[0:4, :].astype(BF)
        rt[1, a] = rows8[4:8, :].astype(BF)
        for dx, dc in x_peers:
            k = dx * 2 + dc
            cc = core_of(dc)
            send(
                rt.at[cc, a], rb[a].at[k], ts_sem.at[k, a], tr_sem.at[k, a],
                dev(mod(x + dx, NX), h, y, zl, cc),
            )
        rb[a][0] = rt[c, a]

    ran_mine, ran_twin = ord_ref[sec], ord_ref[twin]

    def fetch(section, a):
        k = mod(x - lax.div(section, jnp.int32(2)) + NX, NX) * 2
        return rb[a][k + c], rb[a][k + other]

    for a in range(2):
        for dx, dc in x_peers:
            k = dx * 2 + dc
            arrive(rb[a].at[k], ts_sem.at[k, a], tr_sem.at[k, a])
        low, high = fetch(ran_twin, a)
        psd[a, :, 0:half] = low
        psd[a, :, half:] = high
        send(psd.at[a], prb.at[a], ts_sem.at[0, a], tr_sem.at[0, a], partner)
    ran_here = mod(ran_mine, 2) == h
    for copy in stores:
        copy.wait()
    for n in range(heads):
        for b in range(2):
            arrive(
                dkv_ref.at[0, :, pl.ds(their_cols[b] + n * HD, HD)], ds_sem.at[b, n], dr_sem.at[b, n]
            )
    for a, out in enumerate((att_ref, dq_ref)):
        low, high = fetch(ran_mine, a)
        arrive(prb.at[a], ts_sem.at[0, a], tr_sem.at[0, a])
        out[0, :, 0:half] = jnp.where(ran_here, low, prb[a, :, 0:half])
        out[0, :, half:] = jnp.where(ran_here, high, prb[a, :, half:])
    for copy in pending:
        copy.wait_send()


def shards(queries, keys_values, enc_len, order, d_out):
    rows, width = queries.shape[1], queries.shape[2]
    keys = keys_values.shape[1]
    half = width // 2
    heads = half // HD
    targets = NY * NZ * 8
    anywhere = pl.BlockSpec(memory_space=pl.ANY)
    vmem = pl.BlockSpec(memory_space=pltpu.VMEM)
    smem = pl.BlockSpec(memory_space=pltpu.SMEM)
    stats = (3, heads, targets)
    bf = lambda *shape: pltpu.VMEM(shape, BF)
    f32 = lambda *shape: pltpu.VMEM(shape, F32)
    dma = lambda *shape: pltpu.SemaphoreType.DMA(shape)
    return pl.pallas_call(
        kernel,
        out_shape=(
            jax.ShapeDtypeStruct(queries.shape, BF),
            jax.ShapeDtypeStruct(queries.shape, BF),
            jax.ShapeDtypeStruct(keys_values.shape, BF),
        ),
        in_specs=[anywhere, anywhere, smem, smem, anywhere],
        out_specs=(vmem, vmem, anywhere),
        scratch_shapes=[
            bf(2, rows, width),
            bf(2 * NX, rows, half),
            bf(2 * NX, rows, half),
            f32(8, half),
            bf(2, 8, half),
            bf(2, 8, half),
            bf(2, 8, half),
            bf(NY, NZ, 2, 8, half),
            bf(2, heads, targets, HD),
            bf(2, heads, 2 * keys, HD),
            f32(heads, 2 * keys, targets),
            f32(heads, 2 * keys, targets),
            f32(*stats),
            f32(3, *stats),
            f32(*stats),
            f32(3, *stats),
            f32(*stats),
            f32(*stats),
            bf(heads, 2 * keys, targets),
            bf(heads, 2 * keys, targets),
            f32(2, heads, NY, NZ * 8, HD),
            bf(2, heads, 2, NZ * 8, HD),
            bf(2, heads, NZ * 8, HD),
            bf(2, heads, NZ * 8, HD),
            bf(2, heads, 2, NZ * 8, HD),
            f32(2, NZ, 8, half),
            bf(2, 3, 2, 8, half),
            bf(2, 3, 2, 8, half),
            bf(2, 8, half),
            bf(2, 8, half),
            bf(2, 2, rows, half),
            bf(2 * NX, rows, half),
            bf(2 * NX, rows, half),
            bf(2, rows, width),
            bf(2, rows, width),
            bf(2, heads, 2 * keys, HD),
            dma(4 + 4 * heads),
            dma(2 * NX, 2), dma(2 * NX, 2),
            dma(2, heads), dma(2, heads),
            dma(2), dma(2),
            dma(NZ, 2), dma(NZ, 2),
            dma(3, NZ, 2), dma(3, NZ, 2),
            dma(7), dma(7),
            dma(2, heads, 3), dma(2, heads, 3),
            dma(2, 4), dma(2, 4),
            dma(2 * NX, 2), dma(2 * NX, 2),
            dma(2, heads), dma(2, heads),
        ],
        compiler_params=pltpu.CompilerParams(
            collective_id=0, has_side_effects=True, vmem_limit_bytes=56 * 1024 * 1024
        ),
    )(queries, keys_values, enc_len, order, d_out)


def solution(mesh):
    placed = (
        P("section", "seq", None),
        P("section", "seq", None),
        P("section"),
        P(),
        P("section", "seq", None),
    )
    return jax.shard_map(
        shards,
        mesh=mesh,
        in_specs=placed,
        out_specs=(P("section", "seq", None), P("section", "seq", None), P("section", "seq", None)),
        check_vma=False,
    )
```

```python
import functools
import math

import jax
import jax.numpy as jnp
from jax import lax
from jax.experimental import pallas as pl
from jax.experimental.pallas import tpu as pltpu
from jax.sharding import PartitionSpec as P

MESH = pl.DeviceIdType.MESH
HD = 256
NX, NY, NZ = 4, 4, 8
OFFSETS = (0, 1, -1, 2)
BF = jnp.bfloat16
F32 = jnp.float32


def mod(a, n):
    return lax.rem(a, jnp.int32(n))


def merge(parts):
    top = functools.reduce(jnp.maximum, [p[0] for p in parts])
    scale = [jnp.exp(p[0] - top) for p in parts]
    total = sum(p[1] * s for p, s in zip(parts, scale))
    dots = sum(p[2] * s for p, s in zip(parts, scale))
    return top, total, dots


def kernel(
    q_ref, kv_ref, len_ref, ord_hbm, g_ref,
    att_ref, dq_ref, dkv_ref,
    qv, xb, rows32, sb, own, pb, gb, kvv, krel, ev, dv, st, szc, st2, szq,
    wv, dsv, of, zs, zq, zt, zc, rt, rb, psd, prb, dks, drel, ord_ref,
    load_sem, xs_sem, xr_sem, kvs_sem, kvr_sem, rs_sem, rr_sem, ps_sem, pr_sem, zs_sem, zr_sem,
    ss_sem, sr_sem, bs_sem, br_sem, ts_sem, tr_sem, ds_sem, dr_sem, es_sem, er_sem,
):
    sec = lax.axis_index("section")
    seq = lax.axis_index("seq")
    x, h = lax.div(sec, jnp.int32(2)), mod(sec, 2)
    y, zl, c = lax.div(seq, jnp.int32(16)), mod(lax.div(seq, jnp.int32(2)), NZ), mod(seq, 2)
    rows = q_ref.shape[1]
    width = q_ref.shape[2]
    keys = kv_ref.shape[1]
    nh = width // HD
    score_scale = 1.0 / math.sqrt(HD)
    quad, zin = lax.div(zl, jnp.int32(4)) * 4, mod(zl, 4)
    zx = mod(zl + 4, NZ)
    other = 1 - c
    me = y * 2 + c
    twin = x * 2 + (1 - h)

    def dev(xx, hh, yy, zz, cc):
        return (xx * 2 + hh, (yy * NZ + zz) * 2 + cc)

    def zto(d):
        return quad + mod(zin + d, 4)

    def zfrom(d):
        return quad + mod(zin + 4 - d, 4)

    def slot(r):
        base = zfrom(r % 4)
        return base if r < 4 else mod(base + 4, NZ)

    def ynb(d):
        return mod(y + d + NY, NY)

    def core_of(dc):
        return c if dc == 0 else other

    def cols(b, head):
        return pl.ds(pl.multiple_of(b * width + head * HD, HD), HD)

    def block(yy, cc):
        return pl.ds(pl.multiple_of((yy * 2 + cc) * keys, keys), keys)

    crowd = [(dx, dy, dc) for dx in range(NX) for dy in range(NY) for dc in range(2)]
    others = [t for t in crowd if t != (0, 0, 0)]
    partner = dev(x, 1 - h, y, zx, c)
    pending = []
    local = []

    def send(src, dst, ssem, rsem, target):
        copy = pltpu.make_async_remote_copy(
            src_ref=src, dst_ref=dst, send_sem=ssem, recv_sem=rsem, device_id=target, device_id_type=MESH
        )
        copy.start()
        pending.append(copy)

    def arrive(dst, ssem, rsem):
        pltpu.make_async_remote_copy(
            src_ref=dst, dst_ref=dst, send_sem=ssem, recv_sem=rsem, device_id=partner, device_id_type=MESH
        ).wait_recv()

    barrier = pltpu.get_barrier_semaphore()
    peers = [dev(mod(x + dx, NX), h, ynb(dy), zl, core_of(dc)) for dx, dy, dc in others]
    peers += [dev(x, h, y, zto(d), c) for d in (1, 2, 3)]
    peers += [dev(x, h, y, zx, c), partner]
    for peer in peers:
        pl.semaphore_signal(barrier, inc=1, device_id=peer, device_id_type=MESH)
    load_q = [
        pltpu.make_async_copy(ref.at[0], qv.at[a], load_sem.at[a]) for a, ref in enumerate((q_ref, g_ref))
    ]
    load_order = pltpu.make_async_copy(ord_hbm, ord_ref, load_sem.at[7])
    for copy in load_q + [load_order]:
        copy.start()
    load_kv = [
        pltpu.make_async_copy(kv_ref.at[0, :, cols(b, me)], kvv.at[b, block(y, c)], load_sem.at[2 + b])
        for b in range(2)
    ]
    for copy in load_kv:
        copy.start()
    for copy in load_q + [load_order]:
        copy.wait()
    pl.semaphore_wait(barrier, len(peers))

    for k, (dx, dy, dc) in enumerate(crowd):
        if k == 0:
            continue
        head = ynb(dy) * 2 + core_of(dc)
        send(
            qv.at[:, :, cols(0, head)], xb.at[dx, me], xs_sem.at[k], xr_sem.at[k],
            dev(mod(x + dx, NX), h, ynb(dy), zl, core_of(dc)),
        )
    own_copy = pltpu.make_async_copy(qv.at[:, :, cols(0, me)], xb.at[0, me], load_sem.at[4])
    own_copy.start()

    for dc in range(2):
        for b, d in ((0, 1), (1, -1)):
            send(
                kv_ref.at[0, :, cols(b, ynb(2) * 2 + core_of(dc))], krel.at[b, dc], rs_sem.at[b, dc], rr_sem.at[b, dc],
                dev(x, h, ynb(d), zl, core_of(dc)),
            )
    for b in range(2):
        for dyi, dc in ((1, 0), (2, 0), (1, 1), (2, 1), (0, 1)):
            yy = ynb(OFFSETS[dyi])
            send(
                kv_ref.at[0, :, cols(b, yy * 2 + core_of(dc))], kvv.at[b, block(y, c)],
                kvs_sem.at[b, dyi, dc], kvr_sem.at[b, dyi, dc], dev(x, h, yy, zl, core_of(dc)),
            )

    def inverse(section):
        found = jnp.int32(0)
        for k in range(2 * NX):
            found = jnp.where(ord_ref[k] == section, jnp.int32(k), found)
        return found

    src_mine, src_twin = inverse(sec), inverse(twin)

    def steps_to(section):
        return mod(x - lax.div(section, jnp.int32(2)) + NX, NX)

    own_copy.wait()
    for k, (dx, dy, dc) in enumerate(crowd):
        if k:
            arrive(xb.at[dx, ynb(-dy) * 2 + core_of(dc)], xs_sem.at[k], xr_sem.at[k])
    for dst, section in ((sb, src_twin), (own, src_mine)):
        steps = steps_to(section)
        for a in range(2):
            for k in range(nh):
                rows32[a, k * rows : (k + 1) * rows, :] = xb[steps, k, a].astype(F32)
            dst[a] = rows32[a].astype(BF)
        if dst is sb:
            for a in range(2):
                send(sb.at[a], pb.at[a], ps_sem.at[a], pr_sem.at[a], partner)
    mine_here = mod(src_mine, 2) == h

    def to_quad(r, a):
        k = r // 4 * 4
        for d in (1, 3, 2):
            send(
                gb.at[slot(r), a], gb.at[slot(r), a], zs_sem.at[d + k, a], zr_sem.at[d + k, a],
                dev(x, h, y, zto(d), c),
            )

    def z_arrive(r, a):
        arrive(gb.at[slot(r), a], zs_sem.at[r, a], zr_sem.at[r, a])

    for a in range(2):
        arrive(pb.at[a], ps_sem.at[a], pr_sem.at[a])
        gb[zl, a] = jnp.where(mine_here, own[a], pb[a])
        send(gb.at[zl, a], gb.at[zl, a], zs_sem.at[4, a], zr_sem.at[4, a], dev(x, h, y, zx, c))
    for a in range(2):
        to_quad(0, a)
    for dc in range(2):
        for b, d in ((0, 1), (1, -1)):
            arrive(krel.at[b, dc], rs_sem.at[b, dc], rr_sem.at[b, dc])
            send(
                krel.at[b, dc], kvv.at[b, block(ynb(-d), core_of(dc))], kvs_sem.at[b, 3, dc], kvr_sem.at[b, 3, dc],
                dev(x, h, ynb(d), zl, c),
            )
    for a in range(2):
        z_arrive(4, a)
        to_quad(4, a)
    for a in range(2):
        for r in (1, 2, 3, 5, 6, 7):
            z_arrive(r, a)

    targets = NZ * nh * rows
    span = 2 * keys
    key_at = lax.broadcasted_iota(jnp.int32, (span, targets), 0) + zl * span
    nt = (((1,), (1,)), ((), ()))
    nn = (((1,), (0,)), ((), ()))
    tn = (((0,), (0,)), ((), ()))
    query_all = gb[:, 0].reshape(targets, HD)
    grad_all = gb[:, 1].reshape(targets, HD)

    def part(b, j):
        return kvv[b, j * span : (j + 1) * span]

    def kv_arrive(b):
        load_kv[b].wait()
        for dyi, dc in ((0, 1), (1, 0), (1, 1), (2, 0), (2, 1), (3, 0), (3, 1)):
            arrive(kvv.at[b, block(ynb(-OFFSETS[dyi]), core_of(dc))], kvs_sem.at[b, dyi, dc], kvr_sem.at[b, dyi, dc])

    kv_arrive(0)
    top = jnp.full((1, targets), -1e30, F32)
    for j in range(NY):
        scores = lax.dot_general(part(0, j), query_all, nt, preferred_element_type=F32) * score_scale
        scores = jnp.where(key_at + j * NZ * span < len_ref[0], scores, -jnp.inf)
        ev[j] = scores
        top = jnp.maximum(top, jnp.max(scores, axis=0, keepdims=True))
    kv_arrive(1)
    total = jnp.zeros((1, targets), F32)
    dots = jnp.zeros((1, targets), F32)
    for j in range(NY):
        e = jnp.exp(ev[j] - top)
        dp = lax.dot_general(part(1, j), grad_all, nt, preferred_element_type=F32)
        ev[j] = e
        dv[j] = dp
        total = total + jnp.sum(e, axis=0, keepdims=True)
        dots = dots + jnp.sum(e * dp, axis=0, keepdims=True)

    stats = (top, total, dots)
    for i in range(3):
        st[i : i + 1, :] = stats[i]
    send(st, szc, ss_sem.at[0], sr_sem.at[0], dev(x, h, y, zx, c))
    arrive(szc, ss_sem.at[0], sr_sem.at[0])
    stats = merge([stats, [szc[i : i + 1, :] for i in range(3)]])
    for i in range(3):
        st2[i : i + 1, :] = stats[i]
    for d in (1, 3, 2):
        send(st2, szq.at[d - 1], ss_sem.at[d], sr_sem.at[d], dev(x, h, y, zto(d), c))
    for d in (1, 2, 3):
        arrive(szq.at[d - 1], ss_sem.at[d], sr_sem.at[d])
    whole_max, whole_sum, whole_dots = merge(
        [stats] + [[szq[d, i : i + 1, :] for i in range(3)] for d in range(3)]
    )
    inv_sum = 1.0 / whole_sum
    delta = whole_dots * inv_sum
    factor = jnp.exp(st[0:1, :] - whole_max) * inv_sum

    for a in range(2):
        acc = jnp.zeros((targets, HD), F32)
        for j in range(NY):
            p = ev[j] * factor
            if a == 0:
                left = p.astype(BF)
                wv[j] = left
            else:
                left = (p * (dv[j] - delta) * score_scale).astype(BF)
                dsv[j] = left
            acc = acc + lax.dot_general(left, part(1 - a, j), tn, preferred_element_type=F32)
        of[a] = acc.reshape(NZ, nh * rows, HD)
        for d in (1, 3, 2):
            zs[a, d - 1, 0] = of[a, zto(d)].astype(BF)
            zs[a, d - 1, 1] = of[a, mod(zto(d) + 4, NZ)].astype(BF)
            send(zs.at[a, d - 1], zq.at[a, d - 1], bs_sem.at[a, d], br_sem.at[a, d], dev(x, h, y, zto(d), c))

    def piece(b, dyi, dc):
        return dks.at[b, dyi, pl.ds(pl.multiple_of(core_of(dc) * keys, keys), keys)]

    def direct(b, dyi, dc):
        send(
            piece(b, dyi, dc), dkv_ref.at[0, :, cols(b, me)], ds_sem.at[b, dyi, dc], dr_sem.at[b, dyi, dc],
            dev(x, h, ynb(OFFSETS[dyi]), zl, core_of(dc)),
        )

    for dyi in (3, 1, 2, 0):
        j = ynb(OFFSETS[dyi])
        for b in (1, 0):
            right = grad_all if b else query_all
            grad = lax.dot_general((dsv, wv)[b][j], right, nn, preferred_element_type=F32)
            dks[b, dyi] = grad.astype(BF)
            d = 1 if b == 0 else -1
            for dc in range(2):
                if dyi == 3:
                    send(
                        piece(b, dyi, dc), drel.at[b, dc], es_sem.at[b, dc], er_sem.at[b, dc],
                        dev(x, h, ynb(d), zl, core_of(dc)),
                    )
                elif dyi == 0 and dc == 0:
                    copy = pltpu.make_async_copy(piece(b, 0, 0), dkv_ref.at[0, :, cols(b, me)], load_sem.at[5 + b])
                    copy.start()
                    local.append(copy)
                elif b == 1 or dyi == 0:
                    direct(b, dyi, dc)

    for a in range(2):
        for d in (1, 2, 3):
            arrive(zq.at[a, d - 1], bs_sem.at[a, d], br_sem.at[a, d])
        far = of[a, zx] + sum(zq[a, i, 1].astype(F32) for i in range(3))
        zt[a] = far.astype(BF)
        send(zt.at[a], zc.at[a], bs_sem.at[a, 0], br_sem.at[a, 0], dev(x, h, y, zx, c))
    for a in range(2):
        near = of[a, zl] + sum(zq[a, i, 0].astype(F32) for i in range(3))
        arrive(zc.at[a], bs_sem.at[a, 0], br_sem.at[a, 0])
        rows32[a] = near + zc[a].astype(F32)
        for k in range(nh):
            rt[k, a] = rows32[a, k * rows : (k + 1) * rows, :].astype(BF)
    for k, (dx, dy, dc) in enumerate(crowd):
        if k == 0:
            continue
        head = ynb(dy) * 2 + core_of(dc)
        send(
            rt.at[head], rb.at[dx, me], ts_sem.at[k], tr_sem.at[k],
            dev(mod(x + dx, NX), h, ynb(dy), zl, core_of(dc)),
        )
    rb[0, me] = rt[me]
    for dc in range(2):
        for b, d in ((0, 1), (1, -1)):
            arrive(drel.at[b, dc], es_sem.at[b, dc], er_sem.at[b, dc])
            send(
                drel.at[b, dc], dkv_ref.at[0, :, cols(b, ynb(-d) * 2 + core_of(dc))],
                ds_sem.at[b, 3, dc], dr_sem.at[b, 3, dc], dev(x, h, ynb(d), zl, c),
            )
    for dyi in (1, 2):
        for dc in range(2):
            direct(0, dyi, dc)

    for k, (dx, dy, dc) in enumerate(crowd):
        if k:
            arrive(rb.at[dx, ynb(-dy) * 2 + core_of(dc)], ts_sem.at[k], tr_sem.at[k])
    ran_mine, ran_twin = ord_ref[sec], ord_ref[twin]
    steps = steps_to(ran_twin)
    for a in range(2):
        for n in range(nh):
            psd[a, :, n * HD : (n + 1) * HD] = rb[steps, n, a]
    send(psd, prb, ts_sem.at[0], tr_sem.at[0], partner)
    ran_here = mod(ran_mine, 2) == h
    steps = steps_to(ran_mine)
    arrive(prb, ts_sem.at[0], tr_sem.at[0])
    for a, out in enumerate((att_ref, dq_ref)):
        for n in range(nh):
            part_cols = slice(n * HD, (n + 1) * HD)
            out[0, :, part_cols] = jnp.where(ran_here, rb[steps, n, a], prb[a, :, part_cols])
    for copy in local:
        copy.wait()
    for b in range(2):
        for dyi in range(NY):
            for dc in range(2):
                if dyi or dc:
                    head = ynb(-OFFSETS[dyi]) * 2 + core_of(dc)
                    arrive(dkv_ref.at[0, :, cols(b, head)], ds_sem.at[b, dyi, dc], dr_sem.at[b, dyi, dc])
    for copy in pending:
        copy.wait_send()


def writer(*refs):
    ins, outs, sem = refs[:3], refs[3:6], refs[6]
    copies = [pltpu.make_async_copy(i, o, sem.at[n]) for n, (i, o) in enumerate(zip(ins, outs))]
    for copy in copies:
        copy.start()
    for copy in copies:
        copy.wait()


def shards(queries, keys_values, enc_len, order, d_out):
    rows, width = queries.shape[1], queries.shape[2]
    keys = keys_values.shape[1]
    nh = width // HD
    group = nh * rows
    targets = NZ * group
    anywhere = pl.BlockSpec(memory_space=pl.ANY)
    smem = pl.BlockSpec(memory_space=pltpu.SMEM)
    in_hbm = pl.BlockSpec(memory_space=pltpu.HBM)
    vmem = pl.BlockSpec(memory_space=pltpu.VMEM)
    bf = lambda *shape: pltpu.VMEM(shape, BF)
    f32 = lambda *shape: pltpu.VMEM(shape, F32)
    dma = lambda *shape: pltpu.SemaphoreType.DMA(shape)
    shapes = (queries.shape, queries.shape, keys_values.shape)
    pinned = lambda t: pltpu.with_memory_space_constraint(t, pltpu.HBM)
    held = pl.pallas_call(
        kernel,
        out_shape=tuple(pltpu.VMEM(s, BF) for s in shapes),
        in_specs=[in_hbm, in_hbm, smem, in_hbm, in_hbm],
        out_specs=(vmem, vmem, vmem),
        scratch_shapes=[
            bf(2, rows, width),
            bf(NX, nh, 2, rows, HD),
            f32(2, group, HD),
            bf(2, group, HD),
            bf(2, group, HD),
            bf(2, group, HD),
            bf(NZ, 2, group, HD),
            bf(2, 8 * keys, HD),
            bf(2, 2, keys, HD),
            f32(NY, 2 * keys, targets),
            f32(NY, 2 * keys, targets),
            f32(4, targets),
            f32(4, targets),
            f32(4, targets),
            f32(3, 4, targets),
            bf(NY, 2 * keys, targets),
            bf(NY, 2 * keys, targets),
            f32(2, NZ, group, HD),
            bf(2, 3, 2, group, HD),
            bf(2, 3, 2, group, HD),
            bf(2, group, HD),
            bf(2, group, HD),
            bf(nh, 2, rows, HD),
            bf(NX, nh, 2, rows, HD),
            bf(2, rows, width),
            bf(2, rows, width),
            bf(2, NY, 2 * keys, HD),
            bf(2, 2, keys, HD),
            pltpu.SMEM(order.shape, jnp.int32),
            dma(8),
            dma(32), dma(32),
            dma(2, NY, 2), dma(2, NY, 2),
            dma(2, 2), dma(2, 2),
            dma(2), dma(2),
            dma(NZ, 2), dma(NZ, 2),
            dma(4), dma(4),
            dma(2, 4), dma(2, 4),
            dma(32), dma(32),
            dma(2, NY, 2), dma(2, NY, 2),
            dma(2, 2), dma(2, 2),
        ],
        compiler_params=pltpu.CompilerParams(
            collective_id=0, has_side_effects=True, vmem_limit_bytes=48 * 1024 * 1024
        ),
    )(*(pinned(t) if t is not enc_len else t for t in (queries, keys_values, enc_len, order, d_out)))
    return pl.pallas_call(
        writer,
        out_shape=tuple(jax.ShapeDtypeStruct(s, BF) for s in shapes),
        in_specs=[vmem] * 3,
        out_specs=(anywhere,) * 3,
        scratch_shapes=[dma(3)],
    )(*(pltpu.with_memory_space_constraint(t, pltpu.VMEM) for t in held))


def solution(mesh):
    placed = (
        P("section", "seq", None),
        P("section", "seq", None),
        P("section"),
        P(),
        P("section", "seq", None),
    )
    return jax.shard_map(
        shards,
        mesh=mesh,
        in_specs=placed,
        out_specs=(P("section", "seq", None), P("section", "seq", None), P("section", "seq", None)),
        check_vma=False,
    )
```

```python
import functools
import math

import jax
import jax.numpy as jnp
from jax import lax
from jax.experimental import pallas as pl
from jax.experimental.pallas import tpu as pltpu
from jax.sharding import PartitionSpec as P

MESH = pl.DeviceIdType.MESH
HD = 256
NX, NY, NZ = 4, 4, 8
OFFSETS = (0, 1, -1, 2)
BF = jnp.bfloat16
F32 = jnp.float32


def mod(a, n):
    return lax.rem(a, jnp.int32(n))


def merge(parts):
    top = functools.reduce(jnp.maximum, [p[0] for p in parts])
    scale = [jnp.exp(p[0] - top) for p in parts]
    total = sum(p[1] * s for p, s in zip(parts, scale))
    return top, total


def kernel(
    q_ref, kv_ref, len_ref, ord_hbm, g_ref,
    att_ref, dq_ref, dkv_ref,
    qv, xb, rows32, sb, own, pb, gb, kvv, krel, ev, dv, st, szc, st2, szq, dt, dtc, dt2, dtq,
    wv, dsv, of, zs, zq, zt, zc, rt, rb0, rb1, psd, prb, dks, drel, ord_ref,
    load_sem, xs_sem, xr_sem, kvs_sem, kvr_sem, rr_sem, ps_sem, pr_sem, zs_sem, zr_sem,
    ss_sem, sr_sem, bs_sem, br_sem, ts_sem, tr_sem, ds_sem, dr_sem, er_sem,
):
    sec = lax.axis_index("section")
    seq = lax.axis_index("seq")
    x, h = lax.div(sec, jnp.int32(2)), mod(sec, 2)
    y, zl, c = lax.div(seq, jnp.int32(16)), mod(lax.div(seq, jnp.int32(2)), NZ), mod(seq, 2)
    rows = q_ref.shape[1]
    width = q_ref.shape[2]
    keys = kv_ref.shape[1]
    nh = width // HD
    score_scale = 1.0 / math.sqrt(HD)
    quad, zin = lax.div(zl, jnp.int32(4)) * 4, mod(zl, 4)
    zx = mod(zl + 4, NZ)
    other = 1 - c
    rb = (rb0, rb1)
    me = y * 2 + c
    twin = x * 2 + (1 - h)

    def dev(xx, hh, yy, zz, cc):
        return (xx * 2 + hh, (yy * NZ + zz) * 2 + cc)

    def zto(d):
        return quad + mod(zin + d, 4)

    def zfrom(d):
        return quad + mod(zin + 4 - d, 4)

    def slot(r):
        base = zfrom(r % 4)
        return base if r < 4 else mod(base + 4, NZ)

    def ynb(d):
        return mod(y + d + NY, NY)

    def core_of(dc):
        return c if dc == 0 else other

    def cols(b, head):
        return pl.ds(pl.multiple_of(b * width + head * HD, HD), HD)

    def block(b, yy, cc):
        return pl.ds(pl.multiple_of((b * nh + yy * 2 + cc) * keys, keys), keys)

    def pair(b, yy):
        return pl.ds(pl.multiple_of((b * nh + yy * 2) * keys, 2 * keys), 2 * keys)

    crowd = [(dx, dy, dc) for dx in range(NX) for dy in range(NY) for dc in range(2)]
    others = [t for t in crowd if t != (0, 0, 0)]
    partner = dev(x, 1 - h, y, zx, c)
    local = []

    def send(src, dst, ssem, rsem, target):
        copy = pltpu.make_async_remote_copy(
            src_ref=src, dst_ref=dst, send_sem=ssem, recv_sem=rsem, device_id=target, device_id_type=MESH
        )
        copy.start()

    def arrive(dst, rsem):
        pltpu.make_async_remote_copy(
            src_ref=dst, dst_ref=dst, send_sem=tr_sem.at[0, 0], recv_sem=rsem, device_id=partner, device_id_type=MESH
        ).wait_recv()

    def sent(src, ssem):
        pltpu.make_async_remote_copy(
            src_ref=src, dst_ref=src, send_sem=ssem, recv_sem=tr_sem.at[0, 0], device_id=partner, device_id_type=MESH
        ).wait_send()

    barrier = pltpu.get_barrier_semaphore()
    peers = [dev(mod(x + dx, NX), h, ynb(dy), zl, core_of(dc)) for dx, dy, dc in others]
    peers += [dev(x, h, y, zto(d), c) for d in (1, 2, 3)]
    peers += [dev(x, h, y, zx, c), partner]
    for peer in peers:
        pl.semaphore_signal(barrier, inc=1, device_id=peer, device_id_type=MESH)
    load_q = [
        pltpu.make_async_copy(ref.at[0], qv.at[a], load_sem.at[a]) for a, ref in enumerate((q_ref, g_ref))
    ]
    load_order = pltpu.make_async_copy(ord_hbm, ord_ref, load_sem.at[7])
    for copy in load_q + [load_order]:
        copy.start()
    load_kv = [
        pltpu.make_async_copy(kv_ref.at[0, :, cols(b, me)], kvv.at[block(b, y, c)], load_sem.at[2 + b])
        for b in range(2)
    ]
    for copy in load_kv:
        copy.start()
    for copy in load_q + [load_order]:
        copy.wait()
    pl.semaphore_wait(barrier, len(peers))

    for dx, dy, dc in others:
        head = ynb(dy) * 2 + core_of(dc)
        send(
            qv.at[:, :, cols(0, head)], xb.at[dx * nh + me], xs_sem, xr_sem,
            dev(mod(x + dx, NX), h, ynb(dy), zl, core_of(dc)),
        )
    own_copy = pltpu.make_async_copy(qv.at[:, :, cols(0, me)], xb.at[me], load_sem.at[4])
    own_copy.start()

    ways = (1, -1)

    def kv_far(b):
        for dc in range(2):
            send(
                kv_ref.at[0, :, cols(b, ynb(2) * 2 + core_of(dc))], krel.at[b, dc], kvs_sem.at[0], rr_sem.at[b],
                dev(x, h, ynb(ways[dc]), zl, core_of(dc)),
            )

    kv_far(0)
    kv_far(1)

    def kv_direct(b):
        for dyi, dc in ((1, 0), (2, 0), (1, 1), (2, 1), (0, 1)):
            yy = ynb(OFFSETS[dyi])
            send(
                kv_ref.at[0, :, cols(b, yy * 2 + core_of(dc))], kvv.at[block(b, y, c)],
                kvs_sem.at[0], kvr_sem.at[b, dyi], dev(x, h, yy, zl, core_of(dc)),
            )

    def inverse(section):
        found = jnp.int32(0)
        for k in range(2 * NX):
            found = jnp.where(ord_ref[k] == section, jnp.int32(k), found)
        return found

    src_mine, src_twin = inverse(sec), inverse(twin)

    def steps_to(section):
        return mod(x - lax.div(section, jnp.int32(2)) + NX, NX) * nh

    own_copy.wait()
    arrive(xb.at[pl.ds(0, NX * nh - 1)], xr_sem)
    for dst, section in ((sb, src_twin), (own, src_mine)):
        steps = steps_to(section)
        for a in range(2):
            for k in range(nh):
                rows32[a, k * rows : (k + 1) * rows, :] = xb[steps + k, a].astype(F32)
            dst[a] = rows32[a].astype(BF)
            if dst is sb:
                send(sb.at[a], pb.at[a], ps_sem, pr_sem.at[a], partner)
        if dst is sb:
            kv_direct(0)
    mine_here = mod(src_mine, 2) == h

    chunks = [ynb(-d) for d in OFFSETS]

    def kv_arrive(b):
        load_kv[b].wait()
        arrive(kvv.at[block(b, y, other)], kvr_sem.at[b, 0])
        for dyi in (1, 2, 3):
            arrive(kvv.at[pair(b, chunks[dyi])], kvr_sem.at[b, dyi])

    def to_quad(r, a):
        for d in (1, 3, 2):
            send(gb.at[slot(r), a], gb.at[slot(r), a], zs_sem, zr_sem.at[2], dev(x, h, y, zto(d), c))

    for a in range(2):
        arrive(pb.at[a], pr_sem.at[a])
        gb[zl, a] = jnp.where(mine_here, own[a], pb[a])
        send(gb.at[zl, a], gb.at[zl, a], zs_sem, zr_sem.at[a], dev(x, h, y, zx, c))
    for a in range(2):
        to_quad(0, a)
    def kv_forward(b):
        arrive(krel.at[b], rr_sem.at[b])
        for dc, d in enumerate(ways):
            send(
                krel.at[b, dc], kvv.at[block(b, ynb(-d), core_of(dc))], kvs_sem.at[1], kvr_sem.at[b, 3],
                dev(x, h, ynb(d), zl, c),
            )

    kv_forward(0)
    kv_direct(1)
    for a in range(2):
        arrive(gb.at[zx, a], zr_sem.at[a])
        to_quad(4, a)
    kv_forward(1)
    kv_arrive(0)
    arrive(gb.at[pl.ds(0, NZ - 2)], zr_sem.at[2])

    targets = NZ * nh * rows
    span = 2 * keys
    key_at = lax.broadcasted_iota(jnp.int32, (span, targets), 0) + zl * span
    nt = (((1,), (1,)), ((), ()))
    nn = (((1,), (0,)), ((), ()))
    tn = (((0,), (0,)), ((), ()))
    query_all = gb[:, 0].reshape(targets, HD)
    grad_all = gb[:, 1].reshape(targets, HD)

    top = jnp.full((1, targets), -1e30, F32)
    for dyi, j in enumerate(chunks):
        scores = lax.dot_general(kvv[pair(0, j)], query_all, nt, preferred_element_type=F32) * score_scale
        scores = jnp.where(key_at + j * (NZ * span) < len_ref[0], scores, -jnp.inf)
        ev[dyi] = scores
        top = jnp.maximum(top, jnp.max(scores, axis=0, keepdims=True))
    total = jnp.zeros((1, targets), F32)
    for dyi in range(NY):
        e = jnp.exp(ev[dyi] - top)
        ev[dyi] = e
        total = total + jnp.sum(e, axis=0, keepdims=True)

    def put(ref, values):
        for i, value in enumerate(values):
            ref[i : i + 1, :] = value

    put(st, (top, total))
    send(st, szc, ss_sem.at[0], sr_sem.at[0], dev(x, h, y, zx, c))
    arrive(szc, sr_sem.at[0])
    stats = merge([(top, total), (szc[0:1, :], szc[1:2, :])])
    put(st2, stats)
    for d in (1, 3, 2):
        send(st2, szq.at[d - 1], ss_sem.at[0], sr_sem.at[1], dev(x, h, y, zto(d), c))
    kv_arrive(1)
    for dyi, j in enumerate(chunks):
        dv[dyi] = lax.dot_general(kvv[pair(1, j)], grad_all, nt, preferred_element_type=F32)
    arrive(szq.at[pl.ds(0, 3)], sr_sem.at[1])
    whole_max, whole_sum = merge([stats] + [(szq[d, 0:1, :], szq[d, 1:2, :]) for d in range(3)])
    factor = jnp.exp(top - whole_max) / whole_sum

    dots = jnp.zeros((1, targets), F32)
    for dyi in range(NY):
        p = ev[dyi] * factor
        ev[dyi] = p
        wv[dyi] = p.astype(BF)
        dots = dots + jnp.sum(p * dv[dyi], axis=0, keepdims=True)
    dt[...] = jnp.broadcast_to(dots, dt.shape)
    send(dt, dtc, ss_sem.at[1], sr_sem.at[2], dev(x, h, y, zx, c))

    def direct(b, dyi, dc):
        send(
            piece(b, dyi, dc), dkv_ref.at[0, :, cols(b, me)], ds_sem.at[0], dr_sem,
            dev(x, h, ynb(OFFSETS[dyi]), zl, core_of(dc)),
        )

    def piece(b, dyi, dc):
        return dks.at[b, dyi, pl.ds(pl.multiple_of(core_of(dc) * keys, keys), keys)]

    def grads(b):
        left, right = ((dsv, query_all), (wv, grad_all))[b]
        for dyi in (3, 1, 2, 0):
            held = {1: 2, 2: 1}.get(dyi, dyi)
            dks[b, dyi] = lax.dot_general(left[held], right, nn, preferred_element_type=F32).astype(BF)
            for dc in range(2):
                if dyi == 3:
                    send(
                        piece(b, dyi, dc), drel.at[b, dc], ds_sem.at[0], er_sem.at[b],
                        dev(x, h, ynb(ways[dc]), zl, core_of(dc)),
                    )
                elif dyi == 0 and dc == 0:
                    copy = pltpu.make_async_copy(piece(b, 0, 0), dkv_ref.at[0, :, cols(b, me)], load_sem.at[5 + b])
                    copy.start()
                    local.append(copy)
                elif b == 1 or dyi == 0 or dc == 0:
                    direct(b, dyi, dc)

    def forward(b):
        arrive(drel.at[b], er_sem.at[b])
        for dc, d in enumerate(ways):
            send(
                drel.at[b, dc], dkv_ref.at[0, :, cols(b, ynb(-d) * 2 + core_of(dc))],
                ds_sem.at[1], dr_sem, dev(x, h, ynb(d), zl, c),
            )

    def sums(a):
        acc = jnp.zeros((targets, HD), F32)
        for dyi in range(NY):
            j = chunks[dyi]
            acc = acc + lax.dot_general((wv, dsv)[a][dyi], kvv[pair(1 - a, j)], tn, preferred_element_type=F32)
        of[a] = acc.reshape(NZ, nh * rows, HD)
        for d in (1, 3, 2):
            zs[a, d - 1, 0] = of[a, zto(d)].astype(BF)
            zs[a, d - 1, 1] = of[a, mod(zto(d) + 4, NZ)].astype(BF)
            send(zs.at[a, d - 1], zq.at[a, d - 1], bs_sem.at[0], br_sem.at[0, a], dev(x, h, y, zto(d), c))

    def across(a):
        arrive(zq.at[a], br_sem.at[0, a])
        far = of[a, zx] + sum(zq[a, i, 1].astype(F32) for i in range(3))
        zt[a] = far.astype(BF)
        send(zt.at[a], zc.at[a], bs_sem.at[1], br_sem.at[1, a], dev(x, h, y, zx, c))

    def home(a):
        near = of[a, zl] + sum(zq[a, i, 0].astype(F32) for i in range(3))
        arrive(zc.at[a], br_sem.at[1, a])
        rows32[a] = near + zc[a].astype(F32)
        for k in range(nh):
            rt[a, k] = rows32[a, k * rows : (k + 1) * rows, :].astype(BF)
        for dx, dy, dc in others:
            head = ynb(dy) * 2 + core_of(dc)
            send(
                rt.at[a, head], rb[a].at[dx * nh + me], ts_sem.at[0], tr_sem.at[0, a],
                dev(mod(x + dx, NX), h, ynb(dy), zl, core_of(dc)),
            )
        rb[a][me] = rt[a, me]

    ran_mine, ran_twin = ord_ref[sec], ord_ref[twin]

    def over(a):
        arrive(rb[a].at[pl.ds(0, NX * nh - 1)], tr_sem.at[0, a])
        steps = steps_to(ran_twin)
        for n in range(nh):
            psd[a, :, n * HD : (n + 1) * HD] = rb[a][steps + n]
        send(psd.at[a], prb.at[a], ts_sem.at[1], tr_sem.at[1, a], partner)

    def keep(a, out):
        steps = steps_to(ran_mine)
        arrive(prb.at[a], tr_sem.at[1, a])
        for n in range(nh):
            part_cols = slice(n * HD, (n + 1) * HD)
            out[0, :, part_cols] = jnp.where(mod(ran_mine, 2) == h, rb[a][steps + n], prb[a, :, part_cols])

    grads(1)
    sums(0)
    arrive(dtc, sr_sem.at[2])
    dots = dots + dtc[0:1, :]
    dt2[...] = jnp.broadcast_to(dots, dt2.shape)
    for d in (1, 3, 2):
        send(dt2, dtq.at[d - 1], ss_sem.at[1], sr_sem.at[3], dev(x, h, y, zto(d), c))
    across(0)
    arrive(dtq.at[pl.ds(0, 3)], sr_sem.at[3])
    delta = dots + dtq[0, 0:1, :] + dtq[1, 0:1, :] + dtq[2, 0:1, :]
    for dyi in range(NY):
        dsv[dyi] = (ev[dyi] * (dv[dyi] - delta) * score_scale).astype(BF)
    sums(1)
    grads(0)
    forward(1)
    home(0)
    across(1)
    home(1)
    over(0)
    forward(0)
    for dyi in (1, 2):
        direct(0, dyi, 1)
    keep(0, att_ref)
    over(1)
    keep(1, dq_ref)
    sent(xb.at[pl.ds(0, NX * nh - 1)], xs_sem)
    sent(kvv.at[pl.ds(0, 14 * keys)], kvs_sem.at[0])
    sent(kvv.at[pl.ds(0, 4 * keys)], kvs_sem.at[1])
    sent(sb, ps_sem)
    sent(gb.at[pl.ds(0, NZ - 1)], zs_sem)
    sent(szq, ss_sem.at[0])
    sent(dtq, ss_sem.at[1])
    sent(zs, bs_sem.at[0])
    sent(zt, bs_sem.at[1])
    sent(xb.at[pl.ds(0, NX * nh - 1)], ts_sem.at[0])
    sent(psd, ts_sem.at[1])
    for copy in local:
        copy.wait()
    arrive(dkv_ref.at[0, :, pl.ds(0, (2 * nh - 1) * HD - HD)], dr_sem)
    sent(kvv.at[pl.ds(0, 14 * keys)], ds_sem.at[0])
    sent(kvv.at[pl.ds(0, 4 * keys)], ds_sem.at[1])


def writer(*refs):
    ins, outs, sem = refs[:3], refs[3:6], refs[6]
    copies = [pltpu.make_async_copy(i, o, sem.at[n]) for n, (i, o) in enumerate(zip(ins, outs))]
    for copy in copies:
        copy.start()
    for copy in copies:
        copy.wait()


def shards(queries, keys_values, enc_len, order, d_out):
    rows, width = queries.shape[1], queries.shape[2]
    keys = keys_values.shape[1]
    nh = width // HD
    group = nh * rows
    targets = NZ * group
    anywhere = pl.BlockSpec(memory_space=pl.ANY)
    smem = pl.BlockSpec(memory_space=pltpu.SMEM)
    in_hbm = pl.BlockSpec(memory_space=pltpu.HBM)
    vmem = pl.BlockSpec(memory_space=pltpu.VMEM)
    bf = lambda *shape: pltpu.VMEM(shape, BF)
    f32 = lambda *shape: pltpu.VMEM(shape, F32)
    dma = lambda *shape: pltpu.SemaphoreType.DMA(shape)
    one = pltpu.SemaphoreType.DMA
    shapes = (queries.shape, queries.shape, keys_values.shape)
    pinned = lambda t: pltpu.with_memory_space_constraint(t, pltpu.HBM)
    held = pl.pallas_call(
        kernel,
        out_shape=tuple(pltpu.VMEM(s, BF) for s in shapes),
        in_specs=[in_hbm, in_hbm, smem, in_hbm, in_hbm],
        out_specs=(vmem, vmem, vmem),
        scratch_shapes=[
            bf(2, rows, width),
            bf(NX * nh, 2, rows, HD),
            f32(2, group, HD),
            bf(2, group, HD),
            bf(2, group, HD),
            bf(2, group, HD),
            bf(NZ, 2, group, HD),
            bf(2 * nh * keys, HD),
            bf(2, 2, keys, HD),
            f32(NY, 2 * keys, targets),
            f32(NY, 2 * keys, targets),
            f32(2, targets),
            f32(2, targets),
            f32(2, targets),
            f32(4, 2, targets),
            f32(2, targets),
            f32(2, targets),
            f32(2, targets),
            f32(4, 2, targets),
            bf(NY, 2 * keys, targets),
            bf(NY, 2 * keys, targets),
            f32(2, NZ, group, HD),
            bf(2, 3, 2, group, HD),
            bf(2, 3, 2, group, HD),
            bf(2, group, HD),
            bf(2, group, HD),
            bf(2, nh, rows, HD),
            bf(NX * nh, rows, HD),
            bf(NX * nh, rows, HD),
            bf(2, rows, width),
            bf(2, rows, width),
            bf(2, NY, 2 * keys, HD),
            bf(2, 2, keys, HD),
            pltpu.SMEM(order.shape, jnp.int32),
            dma(8),
            one, one,
            dma(2), dma(2, NY), dma(2),
            one, dma(2),
            one, dma(3),
            dma(2), dma(4),
            dma(2), dma(2, 2),
            dma(2), dma(2, 2),
            dma(2), one, dma(2),
        ],
        compiler_params=pltpu.CompilerParams(
            collective_id=0, has_side_effects=True, vmem_limit_bytes=48 * 1024 * 1024
        ),
    )(*(pinned(t) if t is not enc_len else t for t in (queries, keys_values, enc_len, order, d_out)))
    return pl.pallas_call(
        writer,
        out_shape=tuple(jax.ShapeDtypeStruct(s, BF) for s in shapes),
        in_specs=[vmem] * 3,
        out_specs=(anywhere,) * 3,
        scratch_shapes=[dma(3)],
    )(*(pltpu.with_memory_space_constraint(t, pltpu.VMEM) for t in held))


def solution(mesh):
    placed = (
        P("section", "seq", None),
        P("section", "seq", None),
        P("section"),
        P(),
        P("section", "seq", None),
    )
    return jax.shard_map(
        shards,
        mesh=mesh,
        in_specs=placed,
        out_specs=(P("section", "seq", None), P("section", "seq", None), P("section", "seq", None)),
        check_vma=False,
    )
```

```python
import functools
import math

import jax
import jax.numpy as jnp
from jax import lax
from jax.experimental import pallas as pl
from jax.experimental.pallas import tpu as pltpu
from jax.sharding import PartitionSpec as P

MESH = pl.DeviceIdType.MESH
HD = 256
NX, NY, NZ = 4, 4, 8
OFFSETS = (0, 1, -1, 2)
BF = jnp.bfloat16
F32 = jnp.float32


def mod(a, n):
    return lax.rem(a, jnp.int32(n))


def kernel(
    q_ref, kv_ref, len_ref, ord_hbm, g_ref,
    att_ref, dq_ref, dkv_ref,
    qv, xb, rows32, sb, own, pb, gb, kvv, krel, ev, dv, st, szs, dt, dts,
    wv, dsv, of, zs, zq, zt, zc, rt, rb0, rb1, psd, prb, dks, drel, ord_ref,
    load_sem, xs_sem, xr_sem, kvs_sem, kvr_sem, rr_sem, ps_sem, pr_sem, zs_sem, zr_sem,
    ss_sem, sr_sem, bs_sem, br_sem, ts_sem, tr_sem, ds_sem, dr_sem, er_sem,
):
    sec = lax.axis_index("section")
    seq = lax.axis_index("seq")
    x, h = lax.div(sec, jnp.int32(2)), mod(sec, 2)
    y, zl, c = lax.div(seq, jnp.int32(16)), mod(lax.div(seq, jnp.int32(2)), NZ), mod(seq, 2)
    rows = q_ref.shape[1]
    width = q_ref.shape[2]
    keys = kv_ref.shape[1]
    nh = width // HD
    score_scale = 1.0 / math.sqrt(HD)
    quad, zin = lax.div(zl, jnp.int32(4)) * 4, mod(zl, 4)
    zx = mod(zl + 4, NZ)
    other = 1 - c
    rb = (rb0, rb1)
    me = y * 2 + c
    twin = x * 2 + (1 - h)

    def dev(xx, hh, yy, zz, cc):
        return (xx * 2 + hh, (yy * NZ + zz) * 2 + cc)

    def zto(d):
        return quad + mod(zin + d, 4)

    def zfrom(d):
        return quad + mod(zin + 4 - d, 4)

    def zat(r):
        return zto(r % 4) if r < 4 else mod(zto(r % 4) + 4, NZ)

    def slot(r):
        base = zfrom(r % 4)
        return base if r < 4 else mod(base + 4, NZ)

    def ynb(d):
        return mod(y + d + NY, NY)

    def core_of(dc):
        return c if dc == 0 else other

    def cols(b, head):
        return pl.ds(pl.multiple_of(b * width + head * HD, HD), HD)

    def block(b, yy, cc):
        return pl.ds(pl.multiple_of((b * nh + yy * 2 + cc) * keys, keys), keys)

    def pair(b, yy):
        return pl.ds(pl.multiple_of((b * nh + yy * 2) * keys, 2 * keys), 2 * keys)

    crowd = [(dx, dy, dc) for dx in range(NX) for dy in range(NY) for dc in range(2)]
    others = [t for t in crowd if t != (0, 0, 0)]
    partner = dev(x, 1 - h, y, zx, c)
    local = []

    def send(src, dst, ssem, rsem, target):
        copy = pltpu.make_async_remote_copy(
            src_ref=src, dst_ref=dst, send_sem=ssem, recv_sem=rsem, device_id=target, device_id_type=MESH
        )
        copy.start()

    def arrive(dst, rsem):
        pltpu.make_async_remote_copy(
            src_ref=dst, dst_ref=dst, send_sem=tr_sem.at[0, 0], recv_sem=rsem, device_id=partner, device_id_type=MESH
        ).wait_recv()

    def sent(src, ssem):
        pltpu.make_async_remote_copy(
            src_ref=src, dst_ref=src, send_sem=ssem, recv_sem=tr_sem.at[0, 0], device_id=partner, device_id_type=MESH
        ).wait_send()

    barrier = pltpu.get_barrier_semaphore()
    peers = [dev(mod(x + dx, NX), h, ynb(dy), zl, core_of(dc)) for dx, dy, dc in others]
    peers += [dev(x, h, y, zto(d), c) for d in (1, 2, 3)]
    peers += [dev(x, h, y, zx, c), partner]
    for peer in peers:
        pl.semaphore_signal(barrier, inc=1, device_id=peer, device_id_type=MESH)
    load_q = [
        pltpu.make_async_copy(ref.at[0], qv.at[a], load_sem.at[a]) for a, ref in enumerate((q_ref, g_ref))
    ]
    load_order = pltpu.make_async_copy(ord_hbm, ord_ref, load_sem.at[7])
    for copy in load_q + [load_order]:
        copy.start()
    load_kv = [
        pltpu.make_async_copy(kv_ref.at[0, :, cols(b, me)], kvv.at[block(b, y, c)], load_sem.at[2 + b])
        for b in range(2)
    ]
    for copy in load_kv:
        copy.start()
    for copy in load_q + [load_order]:
        copy.wait()
    pl.semaphore_wait(barrier, len(peers))

    for dx, dy, dc in others:
        head = ynb(dy) * 2 + core_of(dc)
        send(
            qv.at[:, :, cols(0, head)], xb.at[dx * nh + me], xs_sem, xr_sem,
            dev(mod(x + dx, NX), h, ynb(dy), zl, core_of(dc)),
        )
    own_copy = pltpu.make_async_copy(qv.at[:, :, cols(0, me)], xb.at[me], load_sem.at[4])
    own_copy.start()

    ways = (1, -1)

    def kv_far(b):
        for dc in range(2):
            send(
                kv_ref.at[0, :, cols(b, ynb(2) * 2 + core_of(dc))], krel.at[b, dc], kvs_sem.at[0], rr_sem.at[b],
                dev(x, h, ynb(ways[dc]), zl, core_of(dc)),
            )

    kv_far(0)
    kv_far(1)

    def kv_direct(b):
        for dyi, dc in ((1, 0), (2, 0), (1, 1), (2, 1), (0, 1)):
            yy = ynb(OFFSETS[dyi])
            send(
                kv_ref.at[0, :, cols(b, yy * 2 + core_of(dc))], kvv.at[block(b, y, c)],
                kvs_sem.at[0], kvr_sem.at[b, dyi], dev(x, h, yy, zl, core_of(dc)),
            )

    def inverse(section):
        found = jnp.int32(0)
        for k in range(2 * NX):
            found = jnp.where(ord_ref[k] == section, jnp.int32(k), found)
        return found

    src_mine, src_twin = inverse(sec), inverse(twin)

    def steps_to(section):
        return mod(x - lax.div(section, jnp.int32(2)) + NX, NX) * nh

    own_copy.wait()
    arrive(xb.at[pl.ds(0, NX * nh - 1)], xr_sem)
    for dst, section in ((sb, src_twin), (own, src_mine)):
        steps = steps_to(section)
        for a in range(2):
            for k in range(nh):
                rows32[a, k * rows : (k + 1) * rows, :] = xb[steps + k, a].astype(F32)
            dst[a] = rows32[a].astype(BF)
            if dst is sb:
                send(sb.at[a], pb.at[a], ps_sem, pr_sem.at[a], partner)
        if dst is sb:
            kv_direct(0)
    mine_here = mod(src_mine, 2) == h

    chunks = [ynb(-d) for d in OFFSETS]

    def kv_arrive(b):
        load_kv[b].wait()
        arrive(kvv.at[block(b, y, other)], kvr_sem.at[b, 0])
        for dyi in (1, 2, 3):
            arrive(kvv.at[pair(b, chunks[dyi])], kvr_sem.at[b, dyi])

    def to_quad(r, a):
        for d in (1, 3, 2):
            send(gb.at[slot(r), a], gb.at[slot(r), a], zs_sem, zr_sem.at[2], dev(x, h, y, zto(d), c))

    for a in range(2):
        arrive(pb.at[a], pr_sem.at[a])
        gb[zl, a] = jnp.where(mine_here, own[a], pb[a])
        send(gb.at[zl, a], gb.at[zl, a], zs_sem, zr_sem.at[a], dev(x, h, y, zx, c))
    for a in range(2):
        to_quad(0, a)
    def kv_forward(b):
        arrive(krel.at[b], rr_sem.at[b])
        for dc, d in enumerate(ways):
            send(
                krel.at[b, dc], kvv.at[block(b, ynb(-d), core_of(dc))], kvs_sem.at[1], kvr_sem.at[b, 3],
                dev(x, h, ynb(d), zl, c),
            )

    kv_forward(0)
    kv_direct(1)
    for a in range(2):
        arrive(gb.at[zx, a], zr_sem.at[a])
        to_quad(4, a)
    kv_forward(1)
    kv_arrive(0)
    arrive(gb.at[pl.ds(0, NZ - 2)], zr_sem.at[2])

    targets = NZ * nh * rows
    span = 2 * keys
    key_at = lax.broadcasted_iota(jnp.int32, (span, targets), 0) + zl * span
    nt = (((1,), (1,)), ((), ()))
    nn = (((1,), (0,)), ((), ()))
    tn = (((0,), (0,)), ((), ()))
    query_all = gb[:, 0].reshape(targets, HD)
    grad_all = gb[:, 1].reshape(targets, HD)

    top = jnp.full((1, targets), -1e30, F32)
    for dyi, j in enumerate(chunks):
        scores = lax.dot_general(kvv[pair(0, j)], query_all, nt, preferred_element_type=F32) * score_scale
        scores = jnp.where(key_at + j * (NZ * span) < len_ref[0], scores, -jnp.inf)
        ev[dyi] = scores
        top = jnp.maximum(top, jnp.max(scores, axis=0, keepdims=True))
    total = jnp.zeros((1, targets), F32)
    for dyi in range(NY):
        e = jnp.exp(ev[dyi] - top)
        ev[dyi] = e
        total = total + jnp.sum(e, axis=0, keepdims=True)

    st[0:1, :] = top
    st[1:2, :] = total
    for r in (7, 5, 6, 4, 3, 2, 1):
        send(st, szs.at[r - 1], ss_sem.at[0], sr_sem.at[0], dev(x, h, y, zat(r), c))
    kv_arrive(1)
    dots = jnp.zeros((1, targets), F32)
    for dyi, j in enumerate(chunks):
        dp = lax.dot_general(kvv[pair(1, j)], grad_all, nt, preferred_element_type=F32)
        dv[dyi] = dp
        dots = dots + jnp.sum(ev[dyi] * dp, axis=0, keepdims=True)
    dt[...] = jnp.broadcast_to(dots, dt.shape)
    for r in (7, 5, 6, 4, 3, 2, 1):
        send(dt, dts.at[r - 1], ss_sem.at[1], sr_sem.at[1], dev(x, h, y, zat(r), c))
    arrive(szs, sr_sem.at[0])
    tops = [top] + [szs[i, 0:1, :] for i in range(NZ - 1)]
    whole_max = functools.reduce(jnp.maximum, tops)
    scales = [jnp.exp(t - whole_max) for t in tops]
    whole_sum = total * scales[0] + sum(szs[i, 1:2, :] * scales[i + 1] for i in range(NZ - 1))
    inv_sum = 1.0 / whole_sum
    factor = scales[0] * inv_sum
    for dyi in range(NY):
        p = ev[dyi] * factor
        ev[dyi] = p
        wv[dyi] = p.astype(BF)

    def direct(b, dyi, dc):
        send(
            piece(b, dyi, dc), dkv_ref.at[0, :, cols(b, me)], ds_sem.at[0], dr_sem,
            dev(x, h, ynb(OFFSETS[dyi]), zl, core_of(dc)),
        )

    def piece(b, dyi, dc):
        return dks.at[b, dyi, pl.ds(pl.multiple_of(core_of(dc) * keys, keys), keys)]

    def grads(b):
        left, right = ((dsv, query_all), (wv, grad_all))[b]
        for dyi in (3, 1, 2, 0):
            held = {1: 2, 2: 1}.get(dyi, dyi)
            dks[b, dyi] = lax.dot_general(left[held], right, nn, preferred_element_type=F32).astype(BF)
            for dc in range(2):
                if dyi == 3:
                    send(
                        piece(b, dyi, dc), drel.at[b, dc], ds_sem.at[0], er_sem.at[b],
                        dev(x, h, ynb(ways[dc]), zl, core_of(dc)),
                    )
                elif dyi == 0 and dc == 0:
                    copy = pltpu.make_async_copy(piece(b, 0, 0), dkv_ref.at[0, :, cols(b, me)], load_sem.at[5 + b])
                    copy.start()
                    local.append(copy)
                elif b == 1 or dyi == 0 or dc == 0:
                    direct(b, dyi, dc)

    def forward(b):
        arrive(drel.at[b], er_sem.at[b])
        for dc, d in enumerate(ways):
            send(
                drel.at[b, dc], dkv_ref.at[0, :, cols(b, ynb(-d) * 2 + core_of(dc))],
                ds_sem.at[1], dr_sem, dev(x, h, ynb(d), zl, c),
            )

    def sums(a):
        acc = jnp.zeros((targets, HD), F32)
        for dyi in range(NY):
            j = chunks[dyi]
            acc = acc + lax.dot_general((wv, dsv)[a][dyi], kvv[pair(1 - a, j)], tn, preferred_element_type=F32)
        of[a] = acc.reshape(NZ, nh * rows, HD)
        for d in (1, 3, 2):
            zs[a, d - 1, 0] = of[a, zto(d)].astype(BF)
            zs[a, d - 1, 1] = of[a, mod(zto(d) + 4, NZ)].astype(BF)
            send(zs.at[a, d - 1], zq.at[a, d - 1], bs_sem.at[0], br_sem.at[0, a], dev(x, h, y, zto(d), c))

    def across(a):
        arrive(zq.at[a], br_sem.at[0, a])
        far = of[a, zx] + sum(zq[a, i, 1].astype(F32) for i in range(3))
        zt[a] = far.astype(BF)
        send(zt.at[a], zc.at[a], bs_sem.at[1], br_sem.at[1, a], dev(x, h, y, zx, c))

    def home(a):
        near = of[a, zl] + sum(zq[a, i, 0].astype(F32) for i in range(3))
        arrive(zc.at[a], br_sem.at[1, a])
        rows32[a] = near + zc[a].astype(F32)
        for k in range(nh):
            rt[a, k] = rows32[a, k * rows : (k + 1) * rows, :].astype(BF)
        for dx, dy, dc in others:
            head = ynb(dy) * 2 + core_of(dc)
            send(
                rt.at[a, head], rb[a].at[dx * nh + me], ts_sem.at[0], tr_sem.at[0, a],
                dev(mod(x + dx, NX), h, ynb(dy), zl, core_of(dc)),
            )
        rb[a][me] = rt[a, me]

    ran_mine, ran_twin = ord_ref[sec], ord_ref[twin]

    def over(a):
        arrive(rb[a].at[pl.ds(0, NX * nh - 1)], tr_sem.at[0, a])
        steps = steps_to(ran_twin)
        for n in range(nh):
            psd[a, :, n * HD : (n + 1) * HD] = rb[a][steps + n]
        send(psd.at[a], prb.at[a], ts_sem.at[1], tr_sem.at[1, a], partner)

    def keep(a, out):
        steps = steps_to(ran_mine)
        arrive(prb.at[a], tr_sem.at[1, a])
        for n in range(nh):
            part_cols = slice(n * HD, (n + 1) * HD)
            out[0, :, part_cols] = jnp.where(mod(ran_mine, 2) == h, rb[a][steps + n], prb[a, :, part_cols])

    grads(1)
    sums(0)
    arrive(dts, sr_sem.at[1])
    delta = dots * scales[0] + sum(dts[i, 0:1, :] * scales[i + 1] for i in range(NZ - 1))
    delta = delta * inv_sum
    for dyi in range(NY):
        dsv[dyi] = (ev[dyi] * (dv[dyi] - delta) * score_scale).astype(BF)
    sums(1)
    across(0)
    grads(0)
    forward(1)
    across(1)
    home(0)
    home(1)
    over(0)
    forward(0)
    for dyi in (1, 2):
        direct(0, dyi, 1)
    over(1)
    keep(0, att_ref)
    keep(1, dq_ref)
    sent(xb.at[pl.ds(0, NX * nh - 1)], xs_sem)
    sent(kvv.at[pl.ds(0, 14 * keys)], kvs_sem.at[0])
    sent(kvv.at[pl.ds(0, 4 * keys)], kvs_sem.at[1])
    sent(sb, ps_sem)
    sent(gb.at[pl.ds(0, NZ - 1)], zs_sem)
    sent(szs, ss_sem.at[0])
    sent(dts, ss_sem.at[1])
    sent(zs, bs_sem.at[0])
    sent(zt, bs_sem.at[1])
    sent(xb.at[pl.ds(0, NX * nh - 1)], ts_sem.at[0])
    sent(psd, ts_sem.at[1])
    for copy in local:
        copy.wait()
    arrive(dkv_ref.at[0, :, pl.ds(0, (2 * nh - 1) * HD - HD)], dr_sem)
    sent(kvv.at[pl.ds(0, 14 * keys)], ds_sem.at[0])
    sent(kvv.at[pl.ds(0, 4 * keys)], ds_sem.at[1])


def writer(*refs):
    ins, outs, sem = refs[:3], refs[3:6], refs[6]
    step = ins[2].shape[1] // 8
    parts = [(ins[2].at[0, pl.ds(i * step, step)], outs[2].at[0, pl.ds(i * step, step)]) for i in range(8)]
    parts += list(zip(ins[:2], outs[:2]))
    copies = [pltpu.make_async_copy(i, o, sem.at[n]) for n, (i, o) in enumerate(parts)]
    for copy in copies:
        copy.start()
    for copy in copies:
        copy.wait()


def shards(queries, keys_values, enc_len, order, d_out):
    rows, width = queries.shape[1], queries.shape[2]
    keys = keys_values.shape[1]
    nh = width // HD
    group = nh * rows
    targets = NZ * group
    anywhere = pl.BlockSpec(memory_space=pl.ANY)
    smem = pl.BlockSpec(memory_space=pltpu.SMEM)
    in_hbm = pl.BlockSpec(memory_space=pltpu.HBM)
    vmem = pl.BlockSpec(memory_space=pltpu.VMEM)
    bf = lambda *shape: pltpu.VMEM(shape, BF)
    f32 = lambda *shape: pltpu.VMEM(shape, F32)
    dma = lambda *shape: pltpu.SemaphoreType.DMA(shape)
    one = pltpu.SemaphoreType.DMA
    shapes = (queries.shape, queries.shape, keys_values.shape)
    pinned = lambda t: pltpu.with_memory_space_constraint(t, pltpu.HBM)
    held = pl.pallas_call(
        kernel,
        out_shape=tuple(pltpu.VMEM(s, BF) for s in shapes),
        in_specs=[in_hbm, in_hbm, smem, in_hbm, in_hbm],
        out_specs=(vmem, vmem, vmem),
        scratch_shapes=[
            bf(2, rows, width),
            bf(NX * nh, 2, rows, HD),
            f32(2, group, HD),
            bf(2, group, HD),
            bf(2, group, HD),
            bf(2, group, HD),
            bf(NZ, 2, group, HD),
            bf(2 * nh * keys, HD),
            bf(2, 2, keys, HD),
            f32(NY, 2 * keys, targets),
            f32(NY, 2 * keys, targets),
            f32(2, targets),
            f32(NZ - 1, 2, targets),
            f32(2, targets),
            f32(NZ - 1, 2, targets),
            bf(NY, 2 * keys, targets),
            bf(NY, 2 * keys, targets),
            f32(2, NZ, group, HD),
            bf(2, 3, 2, group, HD),
            bf(2, 3, 2, group, HD),
            bf(2, group, HD),
            bf(2, group, HD),
            bf(2, nh, rows, HD),
            bf(NX * nh, rows, HD),
            bf(NX * nh, rows, HD),
            bf(2, rows, width),
            bf(2, rows, width),
            bf(2, NY, 2 * keys, HD),
            bf(2, 2, keys, HD),
            pltpu.SMEM(order.shape, jnp.int32),
            dma(8),
            one, one,
            dma(2), dma(2, NY), dma(2),
            one, dma(2),
            one, dma(3),
            dma(2), dma(2),
            dma(2), dma(2, 2),
            dma(2), dma(2, 2),
            dma(2), one, dma(2),
        ],
        compiler_params=pltpu.CompilerParams(
            collective_id=0, has_side_effects=True, vmem_limit_bytes=48 * 1024 * 1024
        ),
    )(*(pinned(t) if t is not enc_len else t for t in (queries, keys_values, enc_len, order, d_out)))
    return pl.pallas_call(
        writer,
        out_shape=tuple(jax.ShapeDtypeStruct(s, BF) for s in shapes),
        in_specs=[vmem] * 3,
        out_specs=(anywhere,) * 3,
        scratch_shapes=[dma(10)],
    )(*(pltpu.with_memory_space_constraint(t, pltpu.VMEM) for t in held))


def solution(mesh):
    placed = (
        P("section", "seq", None),
        P("section", "seq", None),
        P("section"),
        P(),
        P("section", "seq", None),
    )
    return jax.shard_map(
        shards,
        mesh=mesh,
        in_specs=placed,
        out_specs=(P("section", "seq", None), P("section", "seq", None), P("section", "seq", None)),
        check_vma=False,
    )
```

```python
import functools
import math

import jax
import jax.numpy as jnp
from jax import lax
from jax.experimental import pallas as pl
from jax.experimental.pallas import tpu as pltpu
from jax.sharding import PartitionSpec as P

MESH = pl.DeviceIdType.MESH
HD = 256
NX, NY, NZ = 4, 4, 8
OFFSETS = (0, 1, -1, 2)
BF = jnp.bfloat16
F32 = jnp.float32


def mod(a, n):
    return lax.rem(a, jnp.int32(n))


def kernel(
    q_ref, kv_ref, len_ref, ord_hbm, g_ref,
    att_ref, dq_ref, dkv_ref,
    qv, xb, rows32, sb, own, pb, gb, kvv, krel, ev, dv, st, szs, dt, dts,
    wv, dsv, of, zs, zq, zt, zc, rt, rb0, rb1, psd, prb, dks, drel, ord_ref,
    load_sem, xs_sem, xr_sem, kvs_sem, kvr_sem, rr_sem, ps_sem, pr_sem, zs_sem, zr_sem,
    ss_sem, sr_sem, bs_sem, br_sem, ts_sem, tr_sem, ds_sem, dr_sem, er_sem,
):
    sec = lax.axis_index("section")
    seq = lax.axis_index("seq")
    x, h = lax.div(sec, jnp.int32(2)), mod(sec, 2)
    y, zl, c = lax.div(seq, jnp.int32(16)), mod(lax.div(seq, jnp.int32(2)), NZ), mod(seq, 2)
    rows = q_ref.shape[1]
    width = q_ref.shape[2]
    keys = kv_ref.shape[1]
    nh = width // HD
    score_scale = 1.0 / math.sqrt(HD)
    quad, zin = lax.div(zl, jnp.int32(4)) * 4, mod(zl, 4)
    zx = mod(zl + 4, NZ)
    other = 1 - c
    rb = (rb0, rb1)
    me = y * 2 + c
    twin = x * 2 + (1 - h)

    def dev(xx, hh, yy, zz, cc):
        return (xx * 2 + hh, (yy * NZ + zz) * 2 + cc)

    def zto(d):
        return quad + mod(zin + d, 4)

    def zfrom(d):
        return quad + mod(zin + 4 - d, 4)

    def zat(r):
        return zto(r % 4) if r < 4 else mod(zto(r % 4) + 4, NZ)

    def slot(r):
        base = zfrom(r % 4)
        return base if r < 4 else mod(base + 4, NZ)

    def ynb(d):
        return mod(y + d + NY, NY)

    def core_of(dc):
        return c if dc == 0 else other

    def cols(b, head):
        return pl.ds(pl.multiple_of(b * width + head * HD, HD), HD)

    def block(b, yy, cc):
        return pl.ds(pl.multiple_of((b * nh + yy * 2 + cc) * keys, keys), keys)

    def pair(b, yy):
        return pl.ds(pl.multiple_of((b * nh + yy * 2) * keys, 2 * keys), 2 * keys)

    crowd = [(dx, dy, dc) for dx in range(NX) for dy in range(NY) for dc in range(2)]
    others = [t for t in crowd if t != (0, 0, 0)]
    partner = dev(x, 1 - h, y, zx, c)
    local = []

    def send(src, dst, ssem, rsem, target):
        copy = pltpu.make_async_remote_copy(
            src_ref=src, dst_ref=dst, send_sem=ssem, recv_sem=rsem, device_id=target, device_id_type=MESH
        )
        copy.start()

    def arrive(dst, rsem):
        pltpu.make_async_remote_copy(
            src_ref=dst, dst_ref=dst, send_sem=tr_sem.at[0, 0], recv_sem=rsem, device_id=partner, device_id_type=MESH
        ).wait_recv()

    def sent(src, ssem):
        pltpu.make_async_remote_copy(
            src_ref=src, dst_ref=src, send_sem=ssem, recv_sem=tr_sem.at[0, 0], device_id=partner, device_id_type=MESH
        ).wait_send()

    barrier = pltpu.get_barrier_semaphore()
    peers = [dev(mod(x + dx, NX), h, ynb(dy), zl, core_of(dc)) for dx, dy, dc in others]
    peers += [dev(x, h, y, zto(d), c) for d in (1, 2, 3)]
    peers += [dev(x, h, y, zx, c), partner]
    for peer in peers:
        pl.semaphore_signal(barrier, inc=1, device_id=peer, device_id_type=MESH)
    load_q = [
        pltpu.make_async_copy(ref.at[0], qv.at[a], load_sem.at[a]) for a, ref in enumerate((q_ref, g_ref))
    ]
    load_order = pltpu.make_async_copy(ord_hbm, ord_ref, load_sem.at[7])
    for copy in load_q + [load_order]:
        copy.start()
    load_kv = [
        pltpu.make_async_copy(kv_ref.at[0, :, cols(b, me)], kvv.at[block(b, y, c)], load_sem.at[2 + b])
        for b in range(2)
    ]
    for copy in load_kv:
        copy.start()
    for copy in load_q + [load_order]:
        copy.wait()
    pl.semaphore_wait(barrier, len(peers))

    for dx, dy, dc in others:
        head = ynb(dy) * 2 + core_of(dc)
        send(
            qv.at[:, :, cols(0, head)], xb.at[dx * nh + me], xs_sem, xr_sem,
            dev(mod(x + dx, NX), h, ynb(dy), zl, core_of(dc)),
        )
    own_copy = pltpu.make_async_copy(qv.at[:, :, cols(0, me)], xb.at[me], load_sem.at[4])
    own_copy.start()

    ways = (1, -1)

    def kv_far(b):
        for dc in range(2):
            send(
                kv_ref.at[0, :, cols(b, ynb(2) * 2 + core_of(dc))], krel.at[b, dc], kvs_sem.at[0], rr_sem.at[b],
                dev(x, h, ynb(ways[dc]), zl, core_of(dc)),
            )

    kv_far(0)
    kv_far(1)

    def kv_direct(b):
        for dyi, dc in ((1, 0), (2, 0), (1, 1), (2, 1), (0, 1)):
            yy = ynb(OFFSETS[dyi])
            send(
                kv_ref.at[0, :, cols(b, yy * 2 + core_of(dc))], kvv.at[block(b, y, c)],
                kvs_sem.at[0], kvr_sem.at[b, dyi], dev(x, h, yy, zl, core_of(dc)),
            )

    def inverse(section):
        found = jnp.int32(0)
        for k in range(2 * NX):
            found = jnp.where(ord_ref[k] == section, jnp.int32(k), found)
        return found

    src_mine, src_twin = inverse(sec), inverse(twin)

    def steps_to(section):
        return mod(x - lax.div(section, jnp.int32(2)) + NX, NX) * nh

    own_copy.wait()
    arrive(xb.at[pl.ds(0, NX * nh - 1)], xr_sem)
    for dst, section in ((sb, src_twin), (own, src_mine)):
        steps = steps_to(section)
        for a in range(2):
            for k in range(nh):
                rows32[a, k * rows : (k + 1) * rows, :] = xb[steps + k, a].astype(F32)
            dst[a] = rows32[a].astype(BF)
            if dst is sb:
                send(sb.at[a], pb.at[a], ps_sem, pr_sem.at[a], partner)
        if dst is sb:
            kv_direct(0)
    mine_here = mod(src_mine, 2) == h

    chunks = [ynb(-d) for d in OFFSETS]

    def kv_arrive(b):
        load_kv[b].wait()
        arrive(kvv.at[block(b, y, other)], kvr_sem.at[b, 0])
        for dyi in (1, 2, 3):
            arrive(kvv.at[pair(b, chunks[dyi])], kvr_sem.at[b, dyi])

    def to_quad(r, a):
        for d in (1, 3, 2):
            send(gb.at[slot(r), a], gb.at[slot(r), a], zs_sem, zr_sem.at[2], dev(x, h, y, zto(d), c))

    for a in range(2):
        arrive(pb.at[a], pr_sem.at[a])
        gb[zl, a] = jnp.where(mine_here, own[a], pb[a])
        send(gb.at[zl, a], gb.at[zl, a], zs_sem, zr_sem.at[a], dev(x, h, y, zx, c))
    for a in range(2):
        to_quad(0, a)
    def kv_forward(b):
        arrive(krel.at[b], rr_sem.at[b])
        for dc, d in enumerate(ways):
            send(
                krel.at[b, dc], kvv.at[block(b, ynb(-d), core_of(dc))], kvs_sem.at[1], kvr_sem.at[b, 3],
                dev(x, h, ynb(d), zl, c),
            )

    kv_forward(0)
    kv_direct(1)
    for a in range(2):
        arrive(gb.at[zx, a], zr_sem.at[a])
        to_quad(4, a)
    kv_forward(1)
    kv_arrive(0)
    arrive(gb.at[pl.ds(0, NZ - 2)], zr_sem.at[2])

    targets = NZ * nh * rows
    span = 2 * keys
    key_at = lax.broadcasted_iota(jnp.int32, (span, targets), 0) + zl * span
    nt = (((1,), (1,)), ((), ()))
    nn = (((1,), (0,)), ((), ()))
    tn = (((0,), (0,)), ((), ()))
    query_all = gb[:, 0].reshape(targets, HD)
    grad_all = gb[:, 1].reshape(targets, HD)

    top = jnp.full((1, targets), -1e30, F32)
    for dyi, j in enumerate(chunks):
        scores = lax.dot_general(kvv[pair(0, j)], query_all, nt, preferred_element_type=F32) * score_scale
        scores = jnp.where(key_at + j * (NZ * span) < len_ref[0], scores, -jnp.inf)
        ev[dyi] = scores
        top = jnp.maximum(top, jnp.max(scores, axis=0, keepdims=True))
    total = jnp.zeros((1, targets), F32)
    for dyi in range(NY):
        e = jnp.exp(ev[dyi] - top)
        ev[dyi] = e
        total = total + jnp.sum(e, axis=0, keepdims=True)

    st[0:1, :] = top
    st[1:2, :] = total
    for r in (7, 5, 6, 4, 3, 2, 1):
        send(st, szs.at[r - 1], ss_sem.at[0], sr_sem.at[0], dev(x, h, y, zat(r), c))
    kv_arrive(1)
    dots = jnp.zeros((1, targets), F32)
    for dyi, j in enumerate(chunks):
        dp = lax.dot_general(kvv[pair(1, j)], grad_all, nt, preferred_element_type=F32)
        dv[dyi] = dp
        dots = dots + jnp.sum(ev[dyi] * dp, axis=0, keepdims=True)
    dt[...] = jnp.broadcast_to(dots, dt.shape)
    for r in (7, 5, 6, 4, 3, 2, 1):
        send(dt, dts.at[r - 1], ss_sem.at[1], sr_sem.at[1], dev(x, h, y, zat(r), c))
    arrive(szs, sr_sem.at[0])
    tops = [top] + [szs[i, 0:1, :] for i in range(NZ - 1)]
    whole_max = functools.reduce(jnp.maximum, tops)
    scales = [jnp.exp(t - whole_max) for t in tops]
    whole_sum = total * scales[0] + sum(szs[i, 1:2, :] * scales[i + 1] for i in range(NZ - 1))
    inv_sum = 1.0 / whole_sum
    factor = scales[0] * inv_sum
    for dyi in range(NY):
        p = ev[dyi] * factor
        ev[dyi] = p
        wv[dyi] = p.astype(BF)

    def direct(b, dyi, dc):
        send(
            piece(b, dyi, dc), dkv_ref.at[0, :, cols(b, me)], ds_sem.at[0], dr_sem,
            dev(x, h, ynb(OFFSETS[dyi]), zl, core_of(dc)),
        )

    def piece(b, dyi, dc):
        return dks.at[b, dyi, pl.ds(pl.multiple_of(core_of(dc) * keys, keys), keys)]

    def grads(b):
        left, right = ((dsv, query_all), (wv, grad_all))[b]
        for dyi in (3, 1, 2, 0):
            held = {1: 2, 2: 1}.get(dyi, dyi)
            dks[b, dyi] = lax.dot_general(left[held], right, nn, preferred_element_type=F32).astype(BF)
            for dc in range(2):
                if dyi == 3:
                    send(
                        piece(b, dyi, dc), drel.at[b, dc], ds_sem.at[0], er_sem.at[b],
                        dev(x, h, ynb(ways[dc]), zl, core_of(dc)),
                    )
                elif dyi == 0 and dc == 0:
                    copy = pltpu.make_async_copy(piece(b, 0, 0), dkv_ref.at[0, :, cols(b, me)], load_sem.at[5 + b])
                    copy.start()
                    local.append(copy)
                elif b == 1 or dyi == 0:
                    direct(b, dyi, dc)

    def forward(b):
        arrive(drel.at[b], er_sem.at[b])
        for dc, d in enumerate(ways):
            send(
                drel.at[b, dc], dkv_ref.at[0, :, cols(b, ynb(-d) * 2 + core_of(dc))],
                ds_sem.at[1], dr_sem, dev(x, h, ynb(d), zl, c),
            )

    def sums(a):
        acc = jnp.zeros((targets, HD), F32)
        for dyi in range(NY):
            j = chunks[dyi]
            acc = acc + lax.dot_general((wv, dsv)[a][dyi], kvv[pair(1 - a, j)], tn, preferred_element_type=F32)
        of[a] = acc.reshape(NZ, nh * rows, HD)
        for d in (1, 3, 2):
            zs[a, d - 1, 0] = of[a, zto(d)].astype(BF)
            zs[a, d - 1, 1] = of[a, mod(zto(d) + 4, NZ)].astype(BF)
            send(zs.at[a, d - 1], zq.at[a, d - 1], bs_sem.at[0], br_sem.at[0, a], dev(x, h, y, zto(d), c))

    def across(a):
        arrive(zq.at[a], br_sem.at[0, a])
        far = of[a, zx] + sum(zq[a, i, 1].astype(F32) for i in range(3))
        zt[a] = far.astype(BF)
        send(zt.at[a], zc.at[a], bs_sem.at[1], br_sem.at[1, a], dev(x, h, y, zx, c))

    def home(a):
        near = of[a, zl] + sum(zq[a, i, 0].astype(F32) for i in range(3))
        arrive(zc.at[a], br_sem.at[1, a])
        rows32[a] = near + zc[a].astype(F32)
        for k in range(nh):
            rt[a, k] = rows32[a, k * rows : (k + 1) * rows, :].astype(BF)
        for dx, dy, dc in others:
            head = ynb(dy) * 2 + core_of(dc)
            send(
                rt.at[a, head], rb[a].at[dx * nh + me], ts_sem.at[0], tr_sem.at[0, a],
                dev(mod(x + dx, NX), h, ynb(dy), zl, core_of(dc)),
            )
        rb[a][me] = rt[a, me]

    ran_mine, ran_twin = ord_ref[sec], ord_ref[twin]

    def over(a):
        arrive(rb[a].at[pl.ds(0, NX * nh - 1)], tr_sem.at[0, a])
        steps = steps_to(ran_twin)
        for n in range(nh):
            psd[a, :, n * HD : (n + 1) * HD] = rb[a][steps + n]
        send(psd.at[a], prb.at[a], ts_sem.at[1], tr_sem.at[1, a], partner)

    def keep(a, out):
        steps = steps_to(ran_mine)
        arrive(prb.at[a], tr_sem.at[1, a])
        for n in range(nh):
            part_cols = slice(n * HD, (n + 1) * HD)
            out[0, :, part_cols] = jnp.where(mod(ran_mine, 2) == h, rb[a][steps + n], prb[a, :, part_cols])

    grads(1)
    sums(0)
    arrive(dts, sr_sem.at[1])
    delta = dots * scales[0] + sum(dts[i, 0:1, :] * scales[i + 1] for i in range(NZ - 1))
    delta = delta * inv_sum
    for dyi in range(NY):
        dsv[dyi] = (ev[dyi] * (dv[dyi] - delta) * score_scale).astype(BF)
    sums(1)
    across(0)
    grads(0)
    forward(1)
    across(1)
    home(0)
    home(1)
    forward(0)
    for dc in range(2):
        for dyi in (1, 2):
            direct(0, dyi, dc)
    over(0)
    over(1)
    keep(0, att_ref)
    keep(1, dq_ref)
    sent(xb.at[pl.ds(0, NX * nh - 1)], xs_sem)
    sent(kvv.at[pl.ds(0, 14 * keys)], kvs_sem.at[0])
    sent(kvv.at[pl.ds(0, 4 * keys)], kvs_sem.at[1])
    sent(sb, ps_sem)
    sent(gb.at[pl.ds(0, NZ - 1)], zs_sem)
    sent(szs, ss_sem.at[0])
    sent(dts, ss_sem.at[1])
    sent(zs, bs_sem.at[0])
    sent(zt, bs_sem.at[1])
    sent(xb.at[pl.ds(0, NX * nh - 1)], ts_sem.at[0])
    sent(psd, ts_sem.at[1])
    for copy in local:
        copy.wait()
    arrive(dkv_ref.at[0, :, pl.ds(0, (2 * nh - 1) * HD - HD)], dr_sem)
    sent(kvv.at[pl.ds(0, 14 * keys)], ds_sem.at[0])
    sent(kvv.at[pl.ds(0, 4 * keys)], ds_sem.at[1])


def writer(*refs):
    ins, outs, sem = refs[:3], refs[3:6], refs[6]
    step = ins[2].shape[1] // 8
    parts = [(ins[2].at[0, pl.ds(i * step, step)], outs[2].at[0, pl.ds(i * step, step)]) for i in range(8)]
    parts += list(zip(ins[:2], outs[:2]))
    copies = [pltpu.make_async_copy(i, o, sem.at[n]) for n, (i, o) in enumerate(parts)]
    for copy in copies:
        copy.start()
    for copy in copies:
        copy.wait()


def shards(queries, keys_values, enc_len, order, d_out):
    rows, width = queries.shape[1], queries.shape[2]
    keys = keys_values.shape[1]
    nh = width // HD
    group = nh * rows
    targets = NZ * group
    anywhere = pl.BlockSpec(memory_space=pl.ANY)
    smem = pl.BlockSpec(memory_space=pltpu.SMEM)
    in_hbm = pl.BlockSpec(memory_space=pltpu.HBM)
    vmem = pl.BlockSpec(memory_space=pltpu.VMEM)
    bf = lambda *shape: pltpu.VMEM(shape, BF)
    f32 = lambda *shape: pltpu.VMEM(shape, F32)
    dma = lambda *shape: pltpu.SemaphoreType.DMA(shape)
    one = pltpu.SemaphoreType.DMA
    shapes = (queries.shape, queries.shape, keys_values.shape)
    pinned = lambda t: pltpu.with_memory_space_constraint(t, pltpu.HBM)
    held = pl.pallas_call(
        kernel,
        out_shape=tuple(pltpu.VMEM(s, BF) for s in shapes),
        in_specs=[in_hbm, in_hbm, smem, in_hbm, in_hbm],
        out_specs=(vmem, vmem, vmem),
        scratch_shapes=[
            bf(2, rows, width),
            bf(NX * nh, 2, rows, HD),
            f32(2, group, HD),
            bf(2, group, HD),
            bf(2, group, HD),
            bf(2, group, HD),
            bf(NZ, 2, group, HD),
            bf(2 * nh * keys, HD),
            bf(2, 2, keys, HD),
            f32(NY, 2 * keys, targets),
            f32(NY, 2 * keys, targets),
            f32(2, targets),
            f32(NZ - 1, 2, targets),
            f32(2, targets),
            f32(NZ - 1, 2, targets),
            bf(NY, 2 * keys, targets),
            bf(NY, 2 * keys, targets),
            f32(2, NZ, group, HD),
            bf(2, 3, 2, group, HD),
            bf(2, 3, 2, group, HD),
            bf(2, group, HD),
            bf(2, group, HD),
            bf(2, nh, rows, HD),
            bf(NX * nh, rows, HD),
            bf(NX * nh, rows, HD),
            bf(2, rows, width),
            bf(2, rows, width),
            bf(2, NY, 2 * keys, HD),
            bf(2, 2, keys, HD),
            pltpu.SMEM(order.shape, jnp.int32),
            dma(8),
            one, one,
            dma(2), dma(2, NY), dma(2),
            one, dma(2),
            one, dma(3),
            dma(2), dma(2),
            dma(2), dma(2, 2),
            dma(2), dma(2, 2),
            dma(2), one, dma(2),
        ],
        compiler_params=pltpu.CompilerParams(
            collective_id=0, has_side_effects=True, vmem_limit_bytes=48 * 1024 * 1024
        ),
    )(*(pinned(t) if t is not enc_len else t for t in (queries, keys_values, enc_len, order, d_out)))
    return pl.pallas_call(
        writer,
        out_shape=tuple(jax.ShapeDtypeStruct(s, BF) for s in shapes),
        in_specs=[vmem] * 3,
        out_specs=(anywhere,) * 3,
        scratch_shapes=[dma(10)],
    )(*(pltpu.with_memory_space_constraint(t, pltpu.VMEM) for t in held))


def solution(mesh):
    placed = (
        P("section", "seq", None),
        P("section", "seq", None),
        P("section"),
        P(),
        P("section", "seq", None),
    )
    return jax.shard_map(
        shards,
        mesh=mesh,
        in_specs=placed,
        out_specs=(P("section", "seq", None), P("section", "seq", None), P("section", "seq", None)),
        check_vma=False,
    )
```

```python
import functools
import math

import jax
import jax.numpy as jnp
from jax import lax
from jax.experimental import pallas as pl
from jax.experimental.pallas import tpu as pltpu
from jax.sharding import PartitionSpec as P

MESH = pl.DeviceIdType.MESH
HD = 256
NX, NY, NZ = 4, 4, 8
OFFSETS = (0, 1, -1, 2)
BF = jnp.bfloat16
F32 = jnp.float32


def mod(a, n):
    return lax.rem(a, jnp.int32(n))


def kernel(
    q_ref, kv_ref, len_ref, ord_hbm, g_ref,
    att_ref, dq_ref, dkv_ref,
    qv, xb, rows32, sb, own, pb, gb, kvv, krel, ev, dv, st, szs, dt, dts,
    wv, dsv, of, zs, zq, zt, zc, rt, rb0, rb1, psd, prb, dks, drel, ord_ref,
    load_sem, xs_sem, xr_sem, kvs_sem, kvr_sem, rr_sem, ps_sem, pr_sem, zs_sem, zr_sem,
    ss_sem, sr_sem, bs_sem, br_sem, ts_sem, tr_sem, ds_sem, dr_sem, er_sem,
):
    sec = lax.axis_index("section")
    seq = lax.axis_index("seq")
    x, h = lax.div(sec, jnp.int32(2)), mod(sec, 2)
    y, zl, c = lax.div(seq, jnp.int32(16)), mod(lax.div(seq, jnp.int32(2)), NZ), mod(seq, 2)
    rows = q_ref.shape[1]
    width = q_ref.shape[2]
    keys = kv_ref.shape[1]
    nh = width // HD
    score_scale = 1.0 / math.sqrt(HD)
    quad, zin = lax.div(zl, jnp.int32(4)) * 4, mod(zl, 4)
    zx = mod(zl + 4, NZ)
    other = 1 - c
    rb = (rb0, rb1)
    me = y * 2 + c
    twin = x * 2 + (1 - h)

    def dev(xx, hh, yy, zz, cc):
        return (xx * 2 + hh, (yy * NZ + zz) * 2 + cc)

    def zto(d):
        return quad + mod(zin + d, 4)

    def zfrom(d):
        return quad + mod(zin + 4 - d, 4)

    def zat(r):
        return zto(r % 4) if r < 4 else mod(zto(r % 4) + 4, NZ)

    def slot(r):
        base = zfrom(r % 4)
        return base if r < 4 else mod(base + 4, NZ)

    def ynb(d):
        return mod(y + d + NY, NY)

    def core_of(dc):
        return c if dc == 0 else other

    def cols(b, head):
        return pl.ds(pl.multiple_of(b * width + head * HD, HD), HD)

    def block(b, yy, cc):
        return pl.ds(pl.multiple_of((b * nh + yy * 2 + cc) * keys, keys), keys)

    def pair(b, yy):
        return pl.ds(pl.multiple_of((b * nh + yy * 2) * keys, 2 * keys), 2 * keys)

    crowd = [(dx, dy, dc) for dx in range(NX) for dy in range(NY) for dc in range(2)]
    others = [t for t in crowd if t != (0, 0, 0)]
    partner = dev(x, 1 - h, y, zx, c)
    local = []

    def send(src, dst, ssem, rsem, target):
        copy = pltpu.make_async_remote_copy(
            src_ref=src, dst_ref=dst, send_sem=ssem, recv_sem=rsem, device_id=target, device_id_type=MESH
        )
        copy.start()

    def arrive(dst, rsem):
        pltpu.make_async_remote_copy(
            src_ref=dst, dst_ref=dst, send_sem=tr_sem.at[0, 0], recv_sem=rsem, device_id=partner, device_id_type=MESH
        ).wait_recv()

    def sent(src, ssem):
        pltpu.make_async_remote_copy(
            src_ref=src, dst_ref=src, send_sem=ssem, recv_sem=tr_sem.at[0, 0], device_id=partner, device_id_type=MESH
        ).wait_send()

    barrier = pltpu.get_barrier_semaphore()
    peers = [dev(mod(x + dx, NX), h, ynb(dy), zl, core_of(dc)) for dx, dy, dc in others]
    peers += [dev(x, h, y, zto(d), c) for d in (1, 2, 3)]
    peers += [dev(x, h, y, zx, c), partner]
    for peer in peers:
        pl.semaphore_signal(barrier, inc=1, device_id=peer, device_id_type=MESH)
    load_q = [
        pltpu.make_async_copy(ref.at[0], qv.at[a], load_sem.at[a]) for a, ref in enumerate((q_ref, g_ref))
    ]
    load_order = pltpu.make_async_copy(ord_hbm, ord_ref, load_sem.at[7])
    for copy in load_q + [load_order]:
        copy.start()
    load_kv = [
        pltpu.make_async_copy(kv_ref.at[0, :, cols(b, me)], kvv.at[block(b, y, c)], load_sem.at[2 + b])
        for b in range(2)
    ]
    for copy in load_kv:
        copy.start()
    for copy in load_q + [load_order]:
        copy.wait()
    pl.semaphore_wait(barrier, len(peers))

    for dx, dy, dc in others:
        head = ynb(dy) * 2 + core_of(dc)
        send(
            qv.at[:, :, cols(0, head)], xb.at[dx * nh + me], xs_sem, xr_sem,
            dev(mod(x + dx, NX), h, ynb(dy), zl, core_of(dc)),
        )
    own_copy = pltpu.make_async_copy(qv.at[:, :, cols(0, me)], xb.at[me], load_sem.at[4])
    own_copy.start()

    ways = (1, -1)

    def kv_far(b):
        for dc in range(2):
            send(
                kv_ref.at[0, :, cols(b, ynb(2) * 2 + core_of(dc))], krel.at[b, dc], kvs_sem.at[0], rr_sem.at[b],
                dev(x, h, ynb(ways[dc]), zl, core_of(dc)),
            )

    kv_far(0)
    kv_far(1)

    def kv_direct(b):
        for dyi, dc in ((1, 0), (2, 0), (1, 1), (2, 1), (0, 1)):
            yy = ynb(OFFSETS[dyi])
            send(
                kv_ref.at[0, :, cols(b, yy * 2 + core_of(dc))], kvv.at[block(b, y, c)],
                kvs_sem.at[0], kvr_sem.at[b, dyi], dev(x, h, yy, zl, core_of(dc)),
            )

    def inverse(section):
        found = jnp.int32(0)
        for k in range(2 * NX):
            found = jnp.where(ord_ref[k] == section, jnp.int32(k), found)
        return found

    src_mine, src_twin = inverse(sec), inverse(twin)

    def steps_to(section):
        return mod(x - lax.div(section, jnp.int32(2)) + NX, NX) * nh

    own_copy.wait()
    arrive(xb.at[pl.ds(0, NX * nh - 1)], xr_sem)
    for dst, section in ((sb, src_twin), (own, src_mine)):
        steps = steps_to(section)
        for a in range(2):
            for k in range(nh):
                rows32[a, k * rows : (k + 1) * rows, :] = xb[steps + k, a].astype(F32)
            dst[a] = rows32[a].astype(BF)
            if dst is sb:
                send(sb.at[a], pb.at[a], ps_sem, pr_sem.at[a], partner)
        if dst is sb:
            kv_direct(0)
    mine_here = mod(src_mine, 2) == h

    chunks = [ynb(-d) for d in OFFSETS]

    def kv_arrive(b):
        load_kv[b].wait()
        arrive(kvv.at[block(b, y, other)], kvr_sem.at[b, 0])
        for dyi in (1, 2, 3):
            arrive(kvv.at[pair(b, chunks[dyi])], kvr_sem.at[b, dyi])

    def to_quad(r, a):
        for d in (1, 3, 2):
            send(gb.at[slot(r), a], gb.at[slot(r), a], zs_sem, zr_sem.at[2 + a], dev(x, h, y, zto(d), c))

    for a in range(2):
        arrive(pb.at[a], pr_sem.at[a])
        gb[zl, a] = jnp.where(mine_here, own[a], pb[a])
        send(gb.at[zl, a], gb.at[zl, a], zs_sem, zr_sem.at[a], dev(x, h, y, zx, c))
    for a in range(2):
        to_quad(0, a)
    def kv_forward(b):
        arrive(krel.at[b], rr_sem.at[b])
        for dc, d in enumerate(ways):
            send(
                krel.at[b, dc], kvv.at[block(b, ynb(-d), core_of(dc))], kvs_sem.at[1], kvr_sem.at[b, 3],
                dev(x, h, ynb(d), zl, c),
            )

    kv_forward(0)
    kv_direct(1)
    for a in range(2):
        arrive(gb.at[zx, a], zr_sem.at[a])
        to_quad(4, a)
    kv_forward(1)
    kv_arrive(0)
    arrive(gb.at[pl.ds(0, NZ // 2 - 1)], zr_sem.at[2])

    targets = NZ * nh * rows
    span = 2 * keys
    key_at = lax.broadcasted_iota(jnp.int32, (span, targets), 0) + zl * span
    nt = (((1,), (1,)), ((), ()))
    nn = (((1,), (0,)), ((), ()))
    tn = (((0,), (0,)), ((), ()))
    query_all = gb[:, 0].reshape(targets, HD)

    top = jnp.full((1, targets), -1e30, F32)
    for dyi, j in enumerate(chunks):
        scores = lax.dot_general(kvv[pair(0, j)], query_all, nt, preferred_element_type=F32) * score_scale
        scores = jnp.where(key_at + j * (NZ * span) < len_ref[0], scores, -jnp.inf)
        ev[dyi] = scores
        top = jnp.maximum(top, jnp.max(scores, axis=0, keepdims=True))
    total = jnp.zeros((1, targets), F32)
    for dyi in range(NY):
        e = jnp.exp(ev[dyi] - top)
        ev[dyi] = e
        total = total + jnp.sum(e, axis=0, keepdims=True)

    st[0:1, :] = top
    st[1:2, :] = total
    for r in (7, 5, 6, 4, 3, 2, 1):
        send(st, szs.at[r - 1], ss_sem.at[0], sr_sem.at[0], dev(x, h, y, zat(r), c))
    arrive(gb.at[pl.ds(0, NZ // 2 - 1)], zr_sem.at[3])
    grad_all = gb[:, 1].reshape(targets, HD)
    arrive(szs, sr_sem.at[0])
    tops = [top] + [szs[i, 0:1, :] for i in range(NZ - 1)]
    whole_max = functools.reduce(jnp.maximum, tops)
    scales = [jnp.exp(t - whole_max) for t in tops]
    whole_sum = total * scales[0] + sum(szs[i, 1:2, :] * scales[i + 1] for i in range(NZ - 1))
    factor = scales[0] / whole_sum
    for dyi in range(NY):
        p = ev[dyi] * factor
        ev[dyi] = p
        wv[dyi] = p.astype(BF)

    def direct(b, dyi, dc):
        send(
            piece(b, dyi, dc), dkv_ref.at[0, :, cols(b, me)], ds_sem.at[0], dr_sem,
            dev(x, h, ynb(OFFSETS[dyi]), zl, core_of(dc)),
        )

    def piece(b, dyi, dc):
        return dks.at[b, dyi, pl.ds(pl.multiple_of(core_of(dc) * keys, keys), keys)]

    def grads(b, steps):
        left, right = ((dsv, query_all), (wv, grad_all))[b]
        for dyi in steps:
            held = {1: 2, 2: 1}.get(dyi, dyi)
            dks[b, dyi] = lax.dot_general(left[held], right, nn, preferred_element_type=F32).astype(BF)
            for dc in range(2):
                if dyi == 3:
                    send(
                        piece(b, dyi, dc), drel.at[b, dc], ds_sem.at[0], er_sem.at[b],
                        dev(x, h, ynb(ways[dc]), zl, core_of(dc)),
                    )
                elif dyi == 0 and dc == 0:
                    copy = pltpu.make_async_copy(piece(b, 0, 0), dkv_ref.at[0, :, cols(b, me)], load_sem.at[5 + b])
                    copy.start()
                    local.append(copy)
                elif b == 1 or dyi == 0:
                    direct(b, dyi, dc)

    def forward(b):
        arrive(drel.at[b], er_sem.at[b])
        for dc, d in enumerate(ways):
            send(
                drel.at[b, dc], dkv_ref.at[0, :, cols(b, ynb(-d) * 2 + core_of(dc))],
                ds_sem.at[1], dr_sem, dev(x, h, ynb(d), zl, c),
            )

    def sums(a):
        acc = jnp.zeros((targets, HD), F32)
        for dyi in range(NY):
            j = chunks[dyi]
            acc = acc + lax.dot_general((wv, dsv)[a][dyi], kvv[pair(1 - a, j)], tn, preferred_element_type=F32)
        of[a] = acc.reshape(NZ, nh * rows, HD)
        for d in (1, 3, 2):
            zs[a, d - 1, 0] = of[a, zto(d)].astype(BF)
            zs[a, d - 1, 1] = of[a, mod(zto(d) + 4, NZ)].astype(BF)
            send(zs.at[a, d - 1], zq.at[a, d - 1], bs_sem.at[0], br_sem.at[0, a], dev(x, h, y, zto(d), c))

    def across(a):
        arrive(zq.at[a], br_sem.at[0, a])
        far = of[a, zx] + sum(zq[a, i, 1].astype(F32) for i in range(3))
        zt[a] = far.astype(BF)
        send(zt.at[a], zc.at[a], bs_sem.at[1], br_sem.at[1, a], dev(x, h, y, zx, c))

    def home(a):
        near = of[a, zl] + sum(zq[a, i, 0].astype(F32) for i in range(3))
        arrive(zc.at[a], br_sem.at[1, a])
        rows32[a] = near + zc[a].astype(F32)
        for k in range(nh):
            rt[a, k] = rows32[a, k * rows : (k + 1) * rows, :].astype(BF)
        for dx, dy, dc in others:
            head = ynb(dy) * 2 + core_of(dc)
            send(
                rt.at[a, head], rb[a].at[dx * nh + me], ts_sem.at[0], tr_sem.at[0, a],
                dev(mod(x + dx, NX), h, ynb(dy), zl, core_of(dc)),
            )
        rb[a][me] = rt[a, me]

    ran_mine, ran_twin = ord_ref[sec], ord_ref[twin]

    def over(a):
        arrive(rb[a].at[pl.ds(0, NX * nh - 1)], tr_sem.at[0, a])
        steps = steps_to(ran_twin)
        for n in range(nh):
            psd[a, :, n * HD : (n + 1) * HD] = rb[a][steps + n]
        send(psd.at[a], prb.at[a], ts_sem.at[1], tr_sem.at[1, a], partner)

    def keep(a, out):
        steps = steps_to(ran_mine)
        arrive(prb.at[a], tr_sem.at[1, a])
        for n in range(nh):
            part_cols = slice(n * HD, (n + 1) * HD)
            out[0, :, part_cols] = jnp.where(mod(ran_mine, 2) == h, rb[a][steps + n], prb[a, :, part_cols])

    grads(1, (3, 1))
    kv_arrive(1)
    dots = jnp.zeros((1, targets), F32)
    for dyi, j in enumerate(chunks):
        dp = lax.dot_general(kvv[pair(1, j)], grad_all, nt, preferred_element_type=F32)
        dv[dyi] = dp
        dots = dots + jnp.sum(ev[dyi] * dp, axis=0, keepdims=True)
    dt[...] = jnp.broadcast_to(dots, dt.shape)
    for r in (7, 5, 6, 4, 3, 2, 1):
        send(dt, dts.at[r - 1], ss_sem.at[1], sr_sem.at[1], dev(x, h, y, zat(r), c))
    grads(1, (2, 0))
    sums(0)
    arrive(dts, sr_sem.at[1])
    delta = dots + sum(dts[i, 0:1, :] for i in range(NZ - 1))
    for dyi in range(NY):
        dsv[dyi] = (ev[dyi] * (dv[dyi] - delta) * score_scale).astype(BF)
    sums(1)
    across(0)
    grads(0, (3, 1, 2, 0))
    forward(1)
    across(1)
    home(0)
    home(1)
    forward(0)
    for dc in range(2):
        for dyi in (1, 2):
            direct(0, dyi, dc)
    over(0)
    over(1)
    keep(0, att_ref)
    keep(1, dq_ref)
    sent(xb.at[pl.ds(0, NX * nh - 1)], xs_sem)
    sent(kvv.at[pl.ds(0, 14 * keys)], kvs_sem.at[0])
    sent(kvv.at[pl.ds(0, 4 * keys)], kvs_sem.at[1])
    sent(sb, ps_sem)
    sent(gb.at[pl.ds(0, NZ - 1)], zs_sem)
    sent(szs, ss_sem.at[0])
    sent(dts, ss_sem.at[1])
    sent(zs, bs_sem.at[0])
    sent(zt, bs_sem.at[1])
    sent(xb.at[pl.ds(0, NX * nh - 1)], ts_sem.at[0])
    sent(psd, ts_sem.at[1])
    for copy in local:
        copy.wait()
    arrive(dkv_ref.at[0, :, pl.ds(0, (2 * nh - 1) * HD - HD)], dr_sem)
    sent(kvv.at[pl.ds(0, 14 * keys)], ds_sem.at[0])
    sent(kvv.at[pl.ds(0, 4 * keys)], ds_sem.at[1])


def writer(*refs):
    ins, outs, sem = refs[:3], refs[3:6], refs[6]
    step = ins[2].shape[1] // 8
    parts = [(ins[2].at[0, pl.ds(i * step, step)], outs[2].at[0, pl.ds(i * step, step)]) for i in range(8)]
    parts += list(zip(ins[:2], outs[:2]))
    copies = [pltpu.make_async_copy(i, o, sem.at[n]) for n, (i, o) in enumerate(parts)]
    for copy in copies:
        copy.start()
    for copy in copies:
        copy.wait()


def shards(queries, keys_values, enc_len, order, d_out):
    rows, width = queries.shape[1], queries.shape[2]
    keys = keys_values.shape[1]
    nh = width // HD
    group = nh * rows
    targets = NZ * group
    anywhere = pl.BlockSpec(memory_space=pl.ANY)
    smem = pl.BlockSpec(memory_space=pltpu.SMEM)
    in_hbm = pl.BlockSpec(memory_space=pltpu.HBM)
    vmem = pl.BlockSpec(memory_space=pltpu.VMEM)
    bf = lambda *shape: pltpu.VMEM(shape, BF)
    f32 = lambda *shape: pltpu.VMEM(shape, F32)
    dma = lambda *shape: pltpu.SemaphoreType.DMA(shape)
    one = pltpu.SemaphoreType.DMA
    shapes = (queries.shape, queries.shape, keys_values.shape)
    pinned = lambda t: pltpu.with_memory_space_constraint(t, pltpu.HBM)
    held = pl.pallas_call(
        kernel,
        out_shape=tuple(pltpu.VMEM(s, BF) for s in shapes),
        in_specs=[in_hbm, in_hbm, smem, in_hbm, in_hbm],
        out_specs=(vmem, vmem, vmem),
        scratch_shapes=[
            bf(2, rows, width),
            bf(NX * nh, 2, rows, HD),
            f32(2, group, HD),
            bf(2, group, HD),
            bf(2, group, HD),
            bf(2, group, HD),
            bf(NZ, 2, group, HD),
            bf(2 * nh * keys, HD),
            bf(2, 2, keys, HD),
            f32(NY, 2 * keys, targets),
            f32(NY, 2 * keys, targets),
            f32(2, targets),
            f32(NZ - 1, 2, targets),
            f32(2, targets),
            f32(NZ - 1, 2, targets),
            bf(NY, 2 * keys, targets),
            bf(NY, 2 * keys, targets),
            f32(2, NZ, group, HD),
            bf(2, 3, 2, group, HD),
            bf(2, 3, 2, group, HD),
            bf(2, group, HD),
            bf(2, group, HD),
            bf(2, nh, rows, HD),
            bf(NX * nh, rows, HD),
            bf(NX * nh, rows, HD),
            bf(2, rows, width),
            bf(2, rows, width),
            bf(2, NY, 2 * keys, HD),
            bf(2, 2, keys, HD),
            pltpu.SMEM(order.shape, jnp.int32),
            dma(8),
            one, one,
            dma(2), dma(2, NY), dma(2),
            one, dma(2),
            one, dma(4),
            dma(2), dma(2),
            dma(2), dma(2, 2),
            dma(2), dma(2, 2),
            dma(2), one, dma(2),
        ],
        compiler_params=pltpu.CompilerParams(
            collective_id=0, has_side_effects=True, vmem_limit_bytes=48 * 1024 * 1024
        ),
    )(*(pinned(t) if t is not enc_len else t for t in (queries, keys_values, enc_len, order, d_out)))
    return pl.pallas_call(
        writer,
        out_shape=tuple(jax.ShapeDtypeStruct(s, BF) for s in shapes),
        in_specs=[vmem] * 3,
        out_specs=(anywhere,) * 3,
        scratch_shapes=[dma(10)],
    )(*(pltpu.with_memory_space_constraint(t, pltpu.VMEM) for t in held))


def solution(mesh):
    placed = (
        P("section", "seq", None),
        P("section", "seq", None),
        P("section"),
        P(),
        P("section", "seq", None),
    )
    return jax.shard_map(
        shards,
        mesh=mesh,
        in_specs=placed,
        out_specs=(P("section", "seq", None), P("section", "seq", None), P("section", "seq", None)),
        check_vma=False,
    )
```
